32 devices in a mesh: seq: 16 (over z, x, core), head: 2 (over y).
Axes of the slice: x: 2, y: 2, z: 4, core: 2. Of those that a mesh axis runs over, the one named last changes fastest.
Arguments:
- features: bfloat16 [8, 32, 8, 512], P(None, 'seq', 'head'), may hold values from -540 to 540
- gn_gain: float32 [512], replicated, may hold values from 0.5 to 1.5
- gn_bias: float32 [512], replicated, may hold values from -3 to 3
- conv_weight: bfloat16 [3, 3, 3, 16, 512], replicated, may hold values from -0.0546875 to 0.0546875
- conv_bias: float32 [16], replicated, may hold values from -3 to 3
- patch_weight: bfloat16 [64, 3072], replicated, may hold values from -0.75 to 0.75
- patch_bias: float32 [3072], replicated, may hold values from -3 to 3
- image_mod: float32 [3, 3072], replicated, may hold values from -3 to 3
- w_qkv: bfloat16 [3072, 3, 2048], P('seq', None, 'head'), may hold values from -5 to 5
- text_ids: int32 [512], replicated, may hold values from 0 to 16383
- text_length: int32 [1], replicated, may hold values from 256 to 512
- text_table: bfloat16 [3072, 16384], P('seq'), may hold values from -60 to 60
- text_mod: float32 [2, 3072], P(None, 'seq'), may hold values from -3 to 3
- w_text: bfloat16 [3072, 2, 2048], P('seq', None, 'head'), may hold values from -2 to 2
- w_out: bfloat16 [2048, 3072], P('head'), may hold values from -0.625 to 0.625
- out_bias: float32 [3072], replicated, may hold values from -3 to 3
Outputs:
- block_out: bfloat16 [8, 16, 4, 3072], P(None, 'seq', 'head')
The draws below stay inside these ranges and needn't reach their ends.
All inputs are finite; a program needn't handle non-finite values.
Results may differ from the reference program's by a relative error of at most 0.0089.
Values may be sent and summed in bfloat16 or wider, within the bound.
A program may use at most 128 MiB of HBM per device.

```python
import jax
import jax.numpy as jnp
from jax import lax

D = 3072
HEADS = 16
HD = 128
C_VAE = 512
GN_GROUPS = 32
ZC = 16
VOCAB = 16384
TXT = 512
FRAMES = 8
ROWS = 32
COLS = 8
TOKS = 512


def draw_features(key, part):
    base_key = jax.random.fold_in(key, 11)
    noise_key, chan_key = jax.random.split(base_key, 2)
    shape_all = (FRAMES, ROWS, COLS, C_VAE)
    noise_field = jnp.clip(jax.random.normal(noise_key, shape_all, jnp.float32), -6.0, 6.0)
    row_place = jnp.arange(ROWS, dtype=jnp.float32) / max(ROWS - 1, 1)
    row_scale = jnp.exp(jnp.log(3.0) * row_place)
    col_place = jnp.arange(COLS, dtype=jnp.float32) / max(COLS - 1, 1)
    col_scale = jnp.exp(jnp.log(3.0) * col_place)
    chan_scale = jnp.exp(jnp.log(10.0) * jax.random.uniform(chan_key, (C_VAE,), jnp.float32))
    return (noise_field * row_scale[None, :, None, None] * col_scale[None, None, :, None] * chan_scale).astype(jnp.bfloat16)


def draw_text_table(key, part):
    base_key = jax.random.fold_in(key, 23)
    noise_key, column_key = jax.random.split(base_key, 2)
    noise_field = jnp.clip(jax.random.normal(noise_key, (D, VOCAB), jnp.float32), -6.0, 6.0)
    feature_place = jnp.arange(D, dtype=jnp.float32) / (D - 1)
    feature_scale = jnp.exp(jnp.log(10.0) * feature_place)
    column_scale = jnp.exp(jnp.log(10.0) * jax.random.uniform(column_key, (VOCAB,), jnp.float32))
    return (0.1 * noise_field * feature_scale[:, None] * column_scale[None, :]).astype(jnp.bfloat16)


def draw_w_qkv(key, part):
    base_key = jax.random.fold_in(key, 37)
    noise_key, along_key, column_key, pick_key = jax.random.split(base_key, 4)
    shape_all = (D, 3, HEADS * HD)
    noise_field = 0.07 * jnp.clip(jax.random.normal(noise_key, shape_all, jnp.float32), -6.0, 6.0)
    strength = 7.0
    along = jnp.clip(jax.random.normal(along_key, (D,), jnp.float32), -4.0, 4.0) / D ** 0.5
    columns = jnp.clip(jax.random.normal(column_key, (HEADS, HD), jnp.float32), -3.0, 3.0)
    order = jax.random.permutation(pick_key, HEADS)
    level_list = jnp.array([0.45, 0.7, 1.0], jnp.float32)
    levels = jnp.zeros((HEADS,), jnp.float32).at[order[:3]].set(level_list)
    amplitude = (jnp.sqrt(strength * levels)[:, None] * columns).reshape(HEADS * HD)
    aligned = along[:, None] * amplitude[None, :]
    which_part = jnp.array([1.0, 1.0, 0.0], jnp.float32)
    return (noise_field + aligned[:, None, :] * which_part[None, :, None]).astype(jnp.bfloat16)


def plant(values, stream_key, low, high):
    extent = values.shape
    index_at = [jax.random.randint(jax.random.fold_in(stream_key, axis), (), 0, extent[axis]) for axis in range(len(extent))]
    values = values.at[tuple(index_at)].set(low)
    longest = extent.index(max(extent))
    index_at[longest] = (index_at[longest] + 1) % extent[longest]
    return values.at[tuple(index_at)].set(high)


def raised(drawn, rng, source, target, shards_of, factor):
    owner, partner = [(jnp.arange(drawn.shape[axis_at]) // (drawn.shape[axis_at] // shards_of)).reshape([-1 if axis == axis_at else 1 for axis in range(drawn.ndim)]) for axis_at in (source, target)]
    chosen = jax.random.permutation(rng, shards_of)[partner]
    strong = (owner == chosen) | (owner == (partner + shards_of // 2) % shards_of)
    return jnp.where(strong, factor * drawn, drawn)


def block_levels(own_key, extent, pieces, smallest, largest):
    loudness = 1.0
    for dim, parts in pieces:
        heights = jax.random.uniform(jax.random.fold_in(jax.random.fold_in(own_key, 6), dim), (parts,), jnp.float32, smallest / len(pieces), largest / len(pieces))
        loudness = loudness * jnp.repeat(jnp.exp(heights), extent[dim] // parts).reshape((-1,) + (1,) * (len(extent) - 1 - dim))
    return loudness


def scatter_about(key, dims, deviation, reach, pieces=(), kind=jnp.bfloat16):
    result = deviation * jax.random.normal(key, dims, jnp.float32)
    if pieces:
        result = result * block_levels(key, dims, pieces, -0.22, 0.18)
    return jnp.clip(result, -reach, reach).astype(kind)


def heavy_noise(key, dims, scale, bound, pieces, heavy, kind=jnp.bfloat16):
    result = scale * jax.random.normal(key, dims, jnp.float32)
    if pieces:
        result = result * block_levels(key, dims, pieces, -0.22, 0.18)
    return jnp.clip(raised(result, jax.random.fold_in(key, 3), *heavy), -bound, bound).astype(kind)


def setup_inputs(seed: int = 0) -> dict:
    key_of = jax.random.split(jax.random.key(seed), 17)
    features = draw_features(jax.random.fold_in(key_of[16], 71), 0)
    gn_gain = jnp.clip(1.0 + 0.1 * jax.random.normal(key_of[1], (C_VAE,), jnp.float32), 0.5, 1.5)
    gn_bias = scatter_about(key_of[2], (C_VAE,), 0.5, 3.0, (), jnp.float32)
    conv_weight = scatter_about(key_of[3], (3, 3, 3, ZC, C_VAE), (27 * C_VAE) ** -0.5, 0.0546875)
    conv_bias = scatter_about(key_of[4], (ZC,), 0.5, 3.0, (), jnp.float32)
    patch_weight = scatter_about(key_of[5], (4 * ZC, D), (4 * ZC) ** -0.5, 0.75)
    patch_bias = scatter_about(key_of[6], (D,), 0.5, 3.0, (), jnp.float32)
    image_mod = scatter_about(key_of[7], (3, D), 0.5, 3.0, (), jnp.float32)
    w_qkv = draw_w_qkv(jax.random.fold_in(key_of[16], 71), 0)
    text_ids = plant(jax.random.randint(key_of[9], (TXT,), 0, VOCAB), jax.random.fold_in(key_of[9], 1), 0, VOCAB - 1).astype(jnp.int32)
    text_length = jax.random.randint(key_of[10], (1,), TXT // 2, TXT + 1).astype(jnp.int32)
    text_table = draw_text_table(jax.random.fold_in(key_of[16], 71), 0)
    text_mod = scatter_about(key_of[12], (2, D), 0.5, 3.0, ((1, 16),), jnp.float32)
    w_text = heavy_noise(key_of[13], (D, 2, HEADS * HD), 0.1, 2.0, ((0, 16), (2, 2)), (0, 2, 16, 2.0))
    w_out = scatter_about(key_of[14], (HEADS * HD, D), (2.0 / (HEADS * HD) ** 0.5), 0.625, ((0, 2),))
    out_bias = scatter_about(key_of[15], (D,), 0.5, 3.0, (), jnp.float32)
    return {"features": features, "gn_gain": gn_gain, "gn_bias": gn_bias, "conv_weight": conv_weight, "conv_bias": conv_bias, "patch_weight": patch_weight, "patch_bias": patch_bias, "image_mod": image_mod, "w_qkv": w_qkv, "text_ids": text_ids, "text_length": text_length, "text_table": text_table, "text_mod": text_mod, "w_text": w_text, "w_out": w_out, "out_bias": out_bias}


eps_norm = 1e-06

def patchify(latent):
    frame_count, row_count, col_count, chan_count = latent.shape
    blocks = latent.reshape(frame_count, row_count // 2, 2, col_count // 2, 2, chan_count)
    blocks = blocks.transpose(0, 1, 3, 2, 4, 5)
    return blocks.reshape(frame_count * (row_count // 2) * (col_count // 2), 4 * chan_count)

def embed_tokens(patches, patch_weight, patch_bias, image_mod):
    hidden = jnp.dot(patches, patch_weight, preferred_element_type=jnp.float32) + patch_bias
    center = lax.optimization_barrier(jnp.mean(hidden, axis=1, keepdims=True))
    offset = hidden - center
    spread = lax.optimization_barrier(jnp.mean(offset * offset, axis=1, keepdims=True))
    normed = offset * lax.rsqrt(spread + eps_norm)
    modulated = (normed * (1.0 + image_mod[1]) + image_mod[0]).astype(jnp.bfloat16)
    return (hidden, modulated)

def reference(features, gn_gain, gn_bias, conv_weight, conv_bias, patch_weight, patch_bias, image_mod, w_qkv, text_ids, text_length, text_table, text_mod, w_text, w_out, out_bias):
    values = features.astype(jnp.float32)
    grouped = values.reshape(FRAMES, ROWS, COLS, GN_GROUPS, C_VAE // GN_GROUPS)
    cell_count = FRAMES * ROWS * COLS * (C_VAE // GN_GROUPS)
    group_mean = lax.optimization_barrier(jnp.sum(grouped, axis=(0, 1, 2, 4))) / cell_count
    group_square = lax.optimization_barrier(jnp.sum(grouped * grouped, axis=(0, 1, 2, 4))) / cell_count
    group_scale = lax.rsqrt(group_square - group_mean * group_mean + eps_norm)
    normed = ((grouped - group_mean[:, None]) * group_scale[:, None]).reshape(FRAMES, ROWS, COLS, C_VAE)
    activated = jax.nn.silu(normed * gn_gain + gn_bias).astype(jnp.bfloat16)
    padded = jnp.pad(activated, ((0, 0), (1, 1), (1, 1), (0, 0)))
    padded = jnp.concatenate([padded[:1], padded[:1], padded], axis=0)
    latent_sum = jnp.zeros((FRAMES, ROWS, COLS, ZC), jnp.float32)
    for time_off in range(3):
        for row_off in range(3):
            for col_off in range(3):
                window = padded[time_off:time_off + FRAMES, row_off:row_off + ROWS, col_off:col_off + COLS].astype(jnp.float32)
                kernel = conv_weight[time_off, row_off, col_off].astype(jnp.float32)
                latent_sum = latent_sum + jnp.einsum('fyxc,zc->fyxz', window, kernel)
    latent = (latent_sum + conv_bias).astype(jnp.bfloat16)
    hidden, modulated = embed_tokens(patchify(latent), patch_weight, patch_bias, image_mod)
    qkv = jnp.einsum('nd,dkj->nkj', modulated.astype(jnp.float32), w_qkv.astype(jnp.float32)).astype(jnp.bfloat16)
    context = jnp.take(text_table, text_ids, axis=1).astype(jnp.float32)
    text_mean = lax.optimization_barrier(jnp.sum(context, axis=0)) / D
    text_square = lax.optimization_barrier(jnp.sum(context * context, axis=0)) / D
    text_scale = lax.rsqrt(text_square - text_mean * text_mean + eps_norm)
    text_normed = (context - text_mean) * text_scale * (1.0 + text_mod[1][:, None]) + text_mod[0][:, None]
    text_kv = jnp.einsum('dt,dkj->tkj', text_normed, w_text.astype(jnp.float32), precision=lax.Precision.HIGHEST).astype(jnp.bfloat16)
    all_keys = jnp.concatenate([qkv[:, 1], text_kv[:, 0]], axis=0).reshape(TOKS + TXT, HEADS, HD).transpose(1, 0, 2)
    all_values = jnp.concatenate([qkv[:, 2], text_kv[:, 1]], axis=0).reshape(TOKS + TXT, HEADS, HD).transpose(1, 0, 2)
    queries = qkv[:, 0].reshape(TOKS, HEADS, HD).transpose(1, 0, 2)
    key_valid = jnp.arange(TOKS + TXT, dtype=jnp.int32) < TOKS + text_length[0]

    def one_head(operands):
        query_h, key_h, value_h = operands
        scores = jnp.dot(query_h, key_h.T, preferred_element_type=jnp.float32) / HD
        scores = jnp.where(key_valid[None, :], scores, -1e+30)
        row_top = lax.optimization_barrier(jnp.max(scores, axis=1, keepdims=True))
        probs = jnp.exp(scores - row_top)
        totals = lax.optimization_barrier(jnp.sum(probs, axis=1, keepdims=True))
        return jnp.dot(probs.astype(jnp.bfloat16), value_h, preferred_element_type=jnp.float32) / totals
    attended = lax.map(one_head, (queries, all_keys, all_values))
    attended = attended.transpose(1, 0, 2).reshape(TOKS, HEADS * HD).astype(jnp.bfloat16)
    projected = jnp.dot(attended, w_out, preferred_element_type=jnp.float32) + out_bias
    block_out = (hidden + image_mod[2] * projected).astype(jnp.bfloat16)
    return block_out.reshape(FRAMES, ROWS // 2, COLS // 2, D)
```

```python
import functools

import jax
import jax.numpy as jnp
from jax import lax
from jax.experimental import pallas as pl
from jax.experimental.pallas import tpu as pltpu
from jax.sharding import PartitionSpec as P

HD = 128
GN_GROUPS = 32
CHUNK = 512

eps_norm = 1e-06


MESH = pl.DeviceIdType.MESH


def place_of(index, head_n):
    return (lax.div(index, head_n), lax.rem(index, head_n))


def greet_all(seq_n, head_n):
    count = seq_n * head_n
    me = lax.axis_index("seq") * head_n + lax.axis_index("head")
    barrier = pltpu.get_barrier_semaphore()

    def greet(off, carry):
        pl.semaphore_signal(
            barrier,
            inc=1,
            device_id=place_of(lax.rem(me + off, count), head_n),
            device_id_type=MESH,
        )
        return carry

    lax.fori_loop(1, count, greet, 0)
    pl.semaphore_wait(barrier, count - 1)


def start_share(seq_n, head_n, x_ref, out_ref, local_sem, send_sem, recv_sem):
    count = seq_n * head_n
    me = lax.axis_index("seq") * head_n + lax.axis_index("head")

    def copy(off, slot):
        return pltpu.make_async_remote_copy(
            src_ref=x_ref,
            dst_ref=out_ref.at[slot],
            send_sem=send_sem.at[off],
            recv_sem=recv_sem.at[off],
            device_id=place_of(lax.rem(me + off, count), head_n),
            device_id_type=MESH,
        )

    def send(off, carry):
        copy(off, me).start()
        return carry

    lax.fori_loop(1, count, send, 0)
    own = pltpu.make_async_copy(x_ref, out_ref.at[me], local_sem)
    own.start()

    def finish():
        own.wait()

        def wait(off, carry):
            copy(off, me).wait_send()
            copy(off, lax.rem(me + count - off, count)).wait_recv()
            return carry

        lax.fori_loop(1, count, wait, 0)

    return finish


def share_kernel(seq_n, head_n, x_ref, out_ref, local_sem, send_sem, recv_sem):
    greet_all(seq_n, head_n)
    start_share(seq_n, head_n, x_ref, out_ref, local_sem, send_sem, recv_sem)()


def swap_kernel(seq_n, x_ref, out_ref, local_sem, send_sem, recv_sem):
    me, h = lax.axis_index("seq"), lax.axis_index("head")
    barrier = pltpu.get_barrier_semaphore()

    def greet(off, carry):
        pl.semaphore_signal(
            barrier, inc=1, device_id=(lax.rem(me + off, seq_n), h), device_id_type=MESH
        )
        return carry

    lax.fori_loop(1, seq_n, greet, 0)
    pl.semaphore_wait(barrier, seq_n - 1)

    def copy(off, slot):
        peer = lax.rem(me + off, seq_n)
        return pltpu.make_async_remote_copy(
            src_ref=x_ref.at[peer],
            dst_ref=out_ref.at[slot],
            send_sem=send_sem.at[off],
            recv_sem=recv_sem.at[off],
            device_id=(peer, h),
            device_id_type=MESH,
        )

    def send(off, carry):
        copy(off, me).start()
        return carry

    lax.fori_loop(1, seq_n, send, 0)
    own = pltpu.make_async_copy(x_ref.at[me], out_ref.at[me], local_sem)
    own.start()
    own.wait()

    def wait(off, carry):
        copy(off, me).wait_send()
        copy(off, lax.rem(me + seq_n - off, seq_n)).wait_recv()
        return carry

    lax.fori_loop(1, seq_n, wait, 0)


def swap(x):
    seq_n = lax.axis_size("seq")
    return pl.pallas_call(
        functools.partial(swap_kernel, seq_n),
        out_shape=jax.ShapeDtypeStruct(x.shape, x.dtype),
        in_specs=[pl.BlockSpec(memory_space=pltpu.VMEM)],
        out_specs=pl.BlockSpec(memory_space=pltpu.VMEM),
        scratch_shapes=[
            pltpu.SemaphoreType.DMA,
            pltpu.SemaphoreType.DMA((seq_n,)),
            pltpu.SemaphoreType.DMA((seq_n,)),
        ],
        compiler_params=pltpu.CompilerParams(collective_id=1, has_side_effects=True),
    )(x)


def share(x, collective_id):
    seq_n, head_n = lax.axis_size("seq"), lax.axis_size("head")
    count = seq_n * head_n
    return pl.pallas_call(
        functools.partial(share_kernel, seq_n, head_n),
        out_shape=jax.ShapeDtypeStruct((count, *x.shape), x.dtype),
        in_specs=[pl.BlockSpec(memory_space=pltpu.VMEM)],
        out_specs=pl.BlockSpec(memory_space=pltpu.VMEM),
        scratch_shapes=[
            pltpu.SemaphoreType.DMA,
            pltpu.SemaphoreType.DMA((count,)),
            pltpu.SemaphoreType.DMA((count,)),
        ],
        compiler_params=pltpu.CompilerParams(collective_id=collective_id, has_side_effects=True),
    )(x)


def weights_kernel(
    heads_here,
    group,
    wq_ref,
    wt_ref,
    ctx_ref,
    x_ref,
    w_ref,
    full_ref,
    parts_ref,
    local_sem,
    send_sem,
    recv_sem,
    pass_send,
    pass_recv,
    share_local,
    share_send,
    share_recv,
):
    s, h = lax.axis_index("seq"), lax.axis_index("head")
    mine, place = lax.div(s, group), lax.rem(s, group)
    width = heads_here * HD
    greet_all(lax.axis_size("seq"), lax.axis_size("head"))
    finish_share = start_share(
        lax.axis_size("seq"), lax.axis_size("head"), x_ref, parts_ref, share_local, share_send, share_recv
    )

    def pieces(head, slot):
        out = []
        for i in range(5):
            ref, at = (wq_ref, i) if i < 3 else (wt_ref, i - 3)
            start = pl.multiple_of(at * width + head * HD, HD)
            out.append((ref.at[:, pl.ds(start, HD)], w_ref.at[slot, :, pl.ds(i * HD, HD)]))
        out.append((ctx_ref, full_ref.at[slot]))
        return out

    def first(off, slot):
        head = lax.rem(mine + off, heads_here)
        return [
            pltpu.make_async_remote_copy(
                src_ref=src,
                dst_ref=dst,
                send_sem=send_sem.at[off, i],
                recv_sem=recv_sem.at[off, i],
                device_id=(head * group + place, h),
                device_id_type=MESH,
            )
            for i, (src, dst) in enumerate(pieces(head, slot))
        ]

    def second(off, piece, slot):
        peer = mine * group + lax.rem(place + off, group)
        return [
            pltpu.make_async_remote_copy(
                src_ref=ref.at[slot],
                dst_ref=ref.at[slot],
                send_sem=pass_send.at[off, piece, i],
                recv_sem=pass_recv.at[off, piece, i],
                device_id=(peer, h),
                device_id_type=MESH,
            )
            for i, ref in enumerate((w_ref, full_ref))
        ]

    for off in range(1, heads_here):
        for copy in first(off, s):
            copy.start()
    own = [
        pltpu.make_async_copy(src, dst, local_sem.at[i])
        for i, (src, dst) in enumerate(pieces(mine, s))
    ]
    for copy in own:
        copy.start()
    for copy in own:
        copy.wait()
    for piece in range(heads_here):
        slot = lax.rem(mine + heads_here - piece, heads_here) * group + place
        if piece > 0:
            for copy in first(piece, slot):
                copy.wait_recv()
        for off in range(1, group):
            for copy in second(off, piece, slot):
                copy.start()
    for off in range(1, heads_here):
        for copy in first(off, s):
            copy.wait_send()
    for piece in range(heads_here):
        from_group = lax.rem(mine + heads_here - piece, heads_here) * group
        for off in range(1, group):
            for copy in second(off, piece, from_group + place):
                copy.wait_send()
            for copy in second(off, piece, from_group + lax.rem(place + group - off, group)):
                copy.wait_recv()
    finish_share()


def gather_weights(w_qkv, w_text, own_context, shares):
    seq_n = lax.axis_size("seq")
    depth, _, head_width = w_qkv.shape
    heads_here = head_width // HD
    group = seq_n // heads_here
    count = seq_n * lax.axis_size("head")
    text_count = own_context.shape[1]
    anywhere = pl.BlockSpec(memory_space=pl.ANY)
    sems = pltpu.SemaphoreType.DMA
    return pl.pallas_call(
        functools.partial(weights_kernel, heads_here, group),
        out_shape=(
            jax.ShapeDtypeStruct((seq_n, depth, 5 * HD), w_qkv.dtype),
            jax.ShapeDtypeStruct((seq_n, depth, text_count), own_context.dtype),
            jax.ShapeDtypeStruct((count, *shares.shape), shares.dtype),
        ),
        in_specs=[anywhere] * 3 + [pl.BlockSpec(memory_space=pltpu.VMEM)],
        out_specs=(anywhere, anywhere, pl.BlockSpec(memory_space=pltpu.VMEM)),
        scratch_shapes=[
            sems((6,)),
            sems((heads_here, 6)),
            sems((heads_here, 6)),
            sems((group, heads_here, 2)),
            sems((group, heads_here, 2)),
            sems,
            sems((count,)),
            sems((count,)),
        ],
        compiler_params=pltpu.CompilerParams(collective_id=2, has_side_effects=True),
    )(w_qkv.reshape(depth, 3 * head_width), w_text.reshape(depth, 2 * head_width), own_context, shares)


def group_norm(features, gn_gain, gn_bias, text_mod):
    frame_count, row_count, col_count, chan_count = features.shape
    per_group = chan_count // GN_GROUPS
    values = features.astype(jnp.float32)
    chan_sums = jnp.stack(
        [jnp.sum(values, axis=(0, 1, 2)), jnp.sum(values * values, axis=(0, 1, 2))]
    )
    sums = jnp.sum(chan_sums.reshape(2, GN_GROUPS, per_group), axis=2)
    seq_n, head_n = lax.axis_size("seq"), lax.axis_size("head")
    depth = text_mod.shape[1]
    lines = -(-depth // 128)
    mod = jnp.pad(text_mod, ((0, 0), (0, lines * 128 - depth))).reshape(2 * lines, 128)
    block = jnp.concatenate([jnp.pad(sums, ((0, 0), (0, 128 - GN_GROUPS))), mod], axis=0)
    block = jnp.pad(block, ((0, -block.shape[0] % 8), (0, 0)))
    shared = share(block, 0)
    sums = jnp.sum(shared[:, :2, :GN_GROUPS], axis=0)
    mod = shared.reshape(seq_n, head_n, -1, 128)[:, 0, 2 : 2 + 2 * lines]
    mod = mod.reshape(seq_n, 2, lines * 128)[:, :, :depth]
    mod = mod.transpose(1, 0, 2).reshape(2, seq_n * depth)
    cell_count = (
        frame_count * row_count * col_count * per_group * lax.axis_size("seq") * lax.axis_size("head")
    )
    mean = sums[0] / cell_count
    scale = lax.rsqrt(sums[1] / cell_count - mean * mean + eps_norm)
    mean = jnp.repeat(mean, per_group)
    scale = jnp.repeat(scale, per_group)
    normed = (values - mean) * scale
    return jax.nn.silu(normed * gn_gain + gn_bias).astype(jnp.bfloat16), mod


def join_rims(parts, block_dim, dim, unit):
    size = parts.shape[dim]
    blocks = parts.shape[block_dim]
    core = lax.slice_in_dim(parts, unit, size - unit, axis=dim)
    low = lax.slice_in_dim(parts, 0, unit, axis=dim)
    high = lax.slice_in_dim(parts, size - unit, size, axis=dim)
    low = lax.slice_in_dim(low, 1, blocks, axis=block_dim)
    high = lax.slice_in_dim(high, 0, blocks - 1, axis=block_dim)
    pad_low = [(0, 0)] * parts.ndim
    pad_low[block_dim] = (0, 1)
    pad_low[dim] = (size - 3 * unit, 0)
    pad_high = [(0, 0)] * parts.ndim
    pad_high[block_dim] = (1, 0)
    pad_high[dim] = (0, size - 3 * unit)
    return core + jnp.pad(low, pad_low) + jnp.pad(high, pad_high)


def conv_shares(activated, conv_weight):
    padded = jnp.concatenate([activated[:1], activated[:1], activated], axis=0)
    shares = lax.conv_general_dilated(
        padded[None],
        conv_weight,
        (1, 1, 1),
        ((0, 0), (2, 2), (2, 2)),
        dimension_numbers=("NDHWC", "DHWOI", "NDHWC"),
        preferred_element_type=jnp.float32,
    )[0]
    return shares.reshape(-1, 128)


def all_patches(parts, frame_count, row_count, col_count, conv_bias):
    seq_n, head_n = lax.axis_size("seq"), lax.axis_size("head")
    chans = conv_bias.shape[0]
    parts = parts.reshape(
        seq_n, head_n, frame_count, row_count + 2, (col_count + 2) * chans
    )
    parts = join_rims(join_rims(parts, 0, 3, 1), 1, 4, chans)
    latent = (parts + jnp.tile(conv_bias, col_count)).astype(jnp.bfloat16)
    blocks = latent.reshape(
        seq_n, head_n, frame_count, row_count // 2, 2, col_count // 2, 2 * chans
    )
    blocks = blocks.transpose(0, 1, 2, 3, 5, 4, 6)
    own = frame_count * (row_count // 2) * (col_count // 2)
    return blocks.reshape(seq_n * head_n * own, 4 * chans)


def modulate(patches, patch_weight, patch_bias, image_mod):
    hidden = jnp.dot(patches, patch_weight, preferred_element_type=jnp.float32) + patch_bias
    center = jnp.mean(hidden, axis=1, keepdims=True)
    offset = hidden - center
    spread = jnp.mean(offset * offset, axis=1, keepdims=True)
    normed = offset * lax.rsqrt(spread + eps_norm)
    return (normed * (1.0 + image_mod[1]) + image_mod[0]).astype(jnp.bfloat16)


def body(
    features,
    gn_gain,
    gn_bias,
    conv_weight,
    conv_bias,
    patch_weight,
    patch_bias,
    image_mod,
    w_qkv,
    text_ids,
    text_length,
    text_table,
    text_mod,
    w_text,
    w_out,
    out_bias,
):
    frame_count, row_count, col_count, _ = features.shape
    width_full = patch_weight.shape[1]
    seq_n, head_n = lax.axis_size("seq"), lax.axis_size("head")
    seq_i, head_i = lax.axis_index("seq"), lax.axis_index("head")
    depth, _, head_width = w_qkv.shape
    heads_here = head_width // HD
    group = seq_n // heads_here
    text_count = text_ids.shape[0]

    chosen = (
        lax.broadcasted_iota(jnp.int32, (text_table.shape[1], text_count), 0) == text_ids[None, :]
    ).astype(jnp.bfloat16)
    own_context = jnp.dot(text_table, chosen, preferred_element_type=jnp.float32).astype(
        jnp.bfloat16
    )
    activated, mod = group_norm(features, gn_gain, gn_bias, text_mod)
    shares = conv_shares(activated, conv_weight)
    weights, context, parts = gather_weights(w_qkv, w_text, own_context, shares)
    weights = weights.reshape(width_full, 5 * HD)
    context = context.reshape(width_full, text_count).astype(jnp.float32)
    text_mean = jnp.sum(context, axis=0) / width_full
    text_square = jnp.sum(context * context, axis=0) / width_full
    text_scale = lax.rsqrt(text_square - text_mean * text_mean + eps_norm)
    text_normed = (context - text_mean) * text_scale * (1.0 + mod[1][:, None]) + mod[0][:, None]
    text_high = text_normed.astype(jnp.bfloat16)
    text_low = (text_normed - text_high.astype(jnp.float32)).astype(jnp.bfloat16)
    w_text_flat = weights[:, 3 * HD :]
    text_kv = sum(
        lax.dot_general(
            part, w_text_flat, (((0,), (0,)), ((), ())), preferred_element_type=jnp.float32
        )
        for part in (text_high, text_low)
    ).astype(jnp.bfloat16)

    patches = all_patches(parts, frame_count, row_count, col_count, conv_bias)
    own = patches.shape[0] // (seq_n * head_n)
    part_rows = head_n * own // group
    my_part = seq_i % group
    chunk = min(CHUNK, patches.shape[0])

    def project(rows):
        modulated = modulate(rows, patch_weight, patch_bias, image_mod)
        qkv = jnp.dot(modulated, weights[:, : 3 * HD], preferred_element_type=jnp.float32)
        query, kv = qkv[:, :HD], qkv[:, HD:]
        query = lax.dynamic_index_in_dim(
            query.reshape(-1, group, part_rows, HD), my_part, axis=1, keepdims=False
        )
        return kv.astype(jnp.bfloat16), query.reshape(-1, HD).astype(jnp.bfloat16)

    if chunk == patches.shape[0]:
        image_kv, query = project(patches)
    else:
        image_kv, query = lax.map(project, patches.reshape(-1, chunk, patches.shape[1]))
        image_kv = image_kv.reshape(-1, 2 * HD)
        query = query.reshape(-1, HD)

    keys = jnp.concatenate([image_kv[:, :HD], text_kv[:, :HD]], axis=0)
    vals = jnp.concatenate([image_kv[:, HD:], text_kv[:, HD:]], axis=0)
    key_valid = (
        jnp.arange(keys.shape[0], dtype=jnp.int32) < image_kv.shape[0] + text_length[0]
    )
    scores = (
        lax.dot_general(query, keys, (((1,), (1,)), ((), ())), preferred_element_type=jnp.float32)
        / HD
    )
    scores = jnp.where(key_valid[None, :], scores, -1e30)
    probs = jnp.exp(scores - jnp.max(scores, axis=1, keepdims=True))
    totals = jnp.sum(probs, axis=1, keepdims=True)
    attended = (
        jnp.dot(probs.astype(jnp.bfloat16), vals, preferred_element_type=jnp.float32) / totals
    ).astype(jnp.bfloat16)

    attended = attended.reshape(seq_n, part_rows, HD)
    attended = swap(attended)
    attended = attended.reshape(heads_here, group, part_rows, HD).transpose(1, 2, 0, 3)
    attended = attended.reshape(head_n * own, head_width)
    if head_n == 2:
        halves = jnp.dot(attended, w_out, preferred_element_type=jnp.float32)
        halves = halves.reshape(2, own, width_full)
        away = lax.dynamic_index_in_dim(halves, 1 - head_i, 0, keepdims=False)
        here = lax.dynamic_index_in_dim(halves, head_i, 0, keepdims=False)
        projected = here + lax.ppermute(away, "head", [(0, 1), (1, 0)]) + out_bias
    else:
        projected = (
            lax.psum_scatter(
                jnp.dot(attended, w_out, preferred_element_type=jnp.float32),
                "head",
                scatter_dimension=0,
                tiled=True,
            )
            + out_bias
        )
    own_patches = lax.dynamic_slice_in_dim(patches, (seq_i * head_n + head_i) * own, own, axis=0)
    hidden = jnp.dot(own_patches, patch_weight, preferred_element_type=jnp.float32) + patch_bias
    block_out = (hidden + image_mod[2] * projected).astype(jnp.bfloat16)
    return block_out.reshape(frame_count, row_count // 2, col_count // 2, width_full)


NEAR = 4


def lanes_of(shape):
    return lax.broadcasted_iota(jnp.int32, shape, len(shape) - 1)


def group_sum(values, per_group):
    lane = lanes_of(values.shape)
    width = values.shape[-1]
    step = 1
    while step < per_group:
        above = pltpu.roll(values, width - step, 1)
        below = pltpu.roll(values, step, 1)
        values = values + jnp.where(lax.rem(lax.div(lane, step), 2) == 0, above, below)
        step *= 2
    return values


def split_high_low(values):
    high = values.astype(jnp.bfloat16)
    return high, (values - high.astype(jnp.float32)).astype(jnp.bfloat16)


def dot_f32(a, b):
    return jnp.dot(a, b, preferred_element_type=jnp.float32)


def dot_minor(a, b):
    return lax.dot_general(a, b, (((1,), (1,)), ((), ())), preferred_element_type=jnp.float32)


def fused_kernel(
    seq_n,
    head_n,
    cell_count,
    wt_hbm,
    len_ref,
    x_hbm,
    pw_hbm,
    pb_hbm,
    mod_hbm,
    ids_hbm,
    gain_hbm,
    bias_hbm,
    convw_hbm,
    convb_hbm,
    tmod_hbm,
    ob_hbm,
    table_ref,
    wq_ref,
    wout_ref,
    out_hbm,
    wt_ref,
    out_ref,
    x_raw,
    pw_ref,
    pb_ref,
    mod_ref,
    ids_ref,
    gain_ref,
    bias_ref,
    convw_ref,
    convb_ref,
    tmod_ref,
    ob_ref,
    spots,
    tablev,
    wqv,
    ctx_ref,
    stat_ref,
    gsrc,
    gbuf,
    zown,
    zlow,
    zhigh,
    zside,
    psrc,
    pbuf,
    sbuf,
    cbuf,
    wbuf,
    mbuf,
    fstage,
    fpair,
    fxsend,
    fxbuf,
    fzsend,
    fzbuf,
    ffull,
    tstage,
    txbuf,
    tzsend,
    tzbuf,
    tkv,
    qbuf,
    attsend,
    attrecv,
    proj,
    ysend,
    yrecv,
    hidden_ref,
    woutv,
    in_sem,
    out_sem,
    table_sem,
    wq_sem,
    wout_sem,
    g_send,
    g_recv,
    p_send,
    p_recv,
    s_send,
    s_recv,
    c_send,
    c_recv,
    m_send,
    m_recv,
    h_send,
    h_recv,
    fz_send,
    fz_recv,
    tx_send,
    tx_recv,
    tz_send,
    tz_recv,
    a_send,
    a_recv,
    y_send,
    y_recv,
):
    count = seq_n * head_n
    s, h = lax.axis_index("seq"), lax.axis_index("head")
    me = s * head_n + h
    core = lax.rem(s, 2)
    x = lax.rem(lax.div(s, 2), 2)
    z = lax.div(s, NEAR)
    z_n = seq_n // NEAR
    chip = lax.div(s, 2)
    heads_here = seq_n // 2
    sibling = (s + 1 - 2 * core, h)
    across = (s + 2 - 4 * x, h)
    depth = wt_ref.shape[0]
    width = heads_here * HD
    width_full = pw_ref.shape[1]
    own_rows = psrc.shape[0]

    def remote(src, dst, send, recv, device):
        return pltpu.make_async_remote_copy(
            src_ref=src, dst_ref=dst, send_sem=send, recv_sem=recv, device_id=device, device_id_type=MESH
        )

    pieces = table_sem.shape[0]
    piece = table_ref.shape[1] // pieces

    def table_copy(i):
        at = pl.ds(i * piece, piece)
        return pltpu.make_async_copy(table_ref.at[:, at], tablev.at[:, at], table_sem.at[i])

    wq_copy = pltpu.make_async_copy(wq_ref, wqv, wq_sem)
    wout_copy = pltpu.make_async_copy(wout_ref, woutv, wout_sem)
    small = [
        pltpu.make_async_copy(src, dst, in_sem.at[i])
        for i, (src, dst) in enumerate(
            (
                (x_hbm, x_raw),
                (pw_hbm, pw_ref),
                (pb_hbm, pb_ref),
                (mod_hbm, mod_ref),
                (ids_hbm, ids_ref),
                (gain_hbm, gain_ref),
                (bias_hbm, bias_ref),
                (convw_hbm, convw_ref),
                (convb_hbm, convb_ref),
                (tmod_hbm, tmod_ref),
                (ob_hbm, ob_ref),
                (wt_hbm, wt_ref),
            )
        )
    ]
    barrier = pltpu.get_barrier_semaphore()

    def greet(off, carry):
        pl.semaphore_signal(
            barrier, inc=1, device_id=place_of(lax.rem(me + off, count), head_n), device_id_type=MESH
        )
        return carry

    lax.fori_loop(1, count, greet, 0)

    for copy in small[:5]:
        copy.start()
    wq_copy.start()
    for copy in small[5:]:
        copy.start()

    frames, row_n, col_n, _ = x_raw.shape
    cells = frames * row_n * col_n
    small[0].wait()
    for f in range(frames):
        for r in range(row_n):
            at = (f * row_n + r) * col_n
            spots[at : at + col_n, :] = x_raw[f, r].astype(jnp.float32)
    to_at = lax.broadcasted_iota(jnp.int32, (cells, cells), 0)
    from_at = lax.broadcasted_iota(jnp.int32, (cells, cells), 1)
    wanted = lax.rem(to_at, frames) * (row_n * col_n) + lax.div(to_at, frames)
    values = dot_f32((from_at == wanted).astype(jnp.bfloat16), spots[...].astype(jnp.bfloat16))
    chan_count = values.shape[1]
    lines = chan_count // 128
    per_group = chan_count // GN_GROUPS
    total = jnp.sum(values, axis=0, keepdims=True)
    square = jnp.sum(values * values, axis=0, keepdims=True)
    for j in range(lines):
        gsrc[j : j + 1, :] = total[:, j * 128 : (j + 1) * 128]
        gsrc[lines + j : lines + j + 1, :] = square[:, j * 128 : (j + 1) * 128]
    gbuf[me] = gsrc[...]
    for i in range(pieces):
        table_copy(i).start()

    pl.semaphore_wait(barrier, count - 1)

    def wait_bytes(refs, sem):
        pltpu.make_async_copy(refs, refs, sem).wait()

    def spread(src, buf, send, recv):
        def begin():
            def one(off, carry):
                remote(
                    src, buf.at[me], send, recv, place_of(lax.rem(me + off, count), head_n)
                ).start()
                return carry

            lax.fori_loop(1, count, one, 0)

        def all_of(sem):
            wait_bytes(buf.at[pl.ds(0, count - 1)], sem)

        return begin, lambda: all_of(recv), lambda: all_of(send)

    g_begin, g_arrive, g_sent = spread(gsrc, gbuf, g_send, g_recv)
    p_begin, p_arrive, p_sent = spread(psrc, pbuf, p_send, p_recv)
    g_begin()

    w_copy = remote(wt_hbm, wbuf, m_send.at[0], m_recv.at[0], sibling)
    w_copy.start()

    half = ctx_ref.shape[0]
    small[4].wait()
    ids = ids_ref[:, pl.ds(pl.multiple_of(h * half, 128), half)]
    spot = lax.broadcasted_iota(jnp.int32, (piece, half), 0)

    def look_up(i, found):
        table_copy(i).wait()
        chosen = (spot == ids - i * piece).astype(jnp.bfloat16)
        return found + dot_f32(tablev[:, i * piece : (i + 1) * piece], chosen)

    found = jnp.zeros((depth, half), jnp.float32)
    for i in range(pieces):
        found = look_up(i, found)
    stat_ref[0:1, :] = jnp.sum(found, axis=0, keepdims=True)
    stat_ref[1:2, :] = jnp.sum(found * found, axis=0, keepdims=True)
    ctx_ref[...] = jnp.transpose(found).astype(jnp.bfloat16)

    def stat_go(j, carry):
        to_s, to_h = 2 * lax.div(j, head_n) + h, lax.rem(j, head_n)

        @pl.when((to_s != s) | (to_h != h))
        def _():
            remote(stat_ref, sbuf.at[s], s_send, s_recv, (to_s, to_h)).start()

        return carry

    def stat_wait(sem):
        @pl.when(core == h)
        def _():
            wait_bytes(sbuf.at[pl.ds(0, seq_n - 1)], sem)

        @pl.when(core != h)
        def _():
            wait_bytes(sbuf.at[pl.ds(0, seq_n)], sem)

    lax.fori_loop(0, seq_n, stat_go, 0)
    same = core == h
    slot = jnp.where(same, 0, 1)
    there = 2 * chip + h
    near_copy = remote(ctx_ref, cbuf.at[slot], c_send.at[0], c_recv.at[slot], (there, h))
    far_copy = remote(ctx_ref, cbuf.at[slot], c_send.at[1], c_recv.at[slot], (there, 1 - h))
    far_copy.start()

    @pl.when(core != h)
    def _():
        near_copy.start()

    @pl.when(core == h)
    def _():
        cbuf[0] = ctx_ref[...]
        sbuf[s] = stat_ref[...]

    def own_features(ref, rows):
        both = ref[rows, pl.ds(pl.multiple_of(chip * 2 * depth, 128), 2 * depth)].astype(jnp.float32)
        return jnp.where(core == 0, both[:, :depth], both[:, depth:])

    def feature_mean(ref):
        return jnp.mean(ref[...].astype(jnp.float32), axis=1, keepdims=True)

    for copy in small[1:4]:
        copy.wait()
    gain = 1.0 + own_features(mod_ref, slice(1, 2))
    lines_main = (own_features(pw_ref, slice(None)) - feature_mean(pw_ref)) * gain
    line_bias = (own_features(pb_ref, slice(None)) - feature_mean(pb_ref)) * gain
    line_at = lax.broadcasted_iota(jnp.int32, (16, depth), 0)
    lines_rest = jnp.where(
        line_at == 0, line_bias, jnp.where(line_at == 4, own_features(mod_ref, slice(0, 1)), 0.0)
    )
    lines_all = jnp.concatenate([lines_main, lines_rest, jnp.zeros((16, depth), jnp.float32)], axis=0)
    fold_lhs = jnp.concatenate(split_high_low(lines_all), axis=0)
    fold_rows = fstage.shape[1]
    wq_copy.wait()
    for i in range(3):
        product = dot_f32(fold_lhs, wqv[i])
        product = product[:fold_rows] + product[fold_rows:]
        for hh in range(heads_here):
            fstage[hh, :, i * HD : (i + 1) * HD] = product[:, hh * HD : (hh + 1) * HD]

    rows_half = fpair.shape[1]

    def half_rows(which):
        return pl.ds(pl.multiple_of(which * rows_half, 8), rows_half)

    pair_copy = remote(fstage.at[:, half_rows(1 - core), :], fpair, m_send.at[2], m_recv.at[2], sibling)
    pair_copy.start()

    mod_copy = remote(tmod_ref, mbuf, m_send.at[1], m_recv.at[1], sibling)
    for copy in small[5:]:
        copy.wait()
    mod_copy.start()

    g_arrive()
    sums = group_sum(jnp.sum(gbuf[...], axis=0), per_group) / cell_count
    mean = sums[:lines]
    scale = lax.rsqrt(sums[lines:] - mean * mean + eps_norm)
    mean = jnp.concatenate([mean[j : j + 1] for j in range(lines)], axis=1)
    scale = jnp.concatenate([scale[j : j + 1] for j in range(lines)], axis=1)
    normed = (values - mean) * scale * gain_ref[...] + bias_ref[...]
    active = normed / (1.0 + jnp.exp(-normed))
    frame = lax.rem(lax.broadcasted_iota(jnp.int32, active.shape, 0), frames)
    back_one = jnp.where(frame == 0, active, pltpu.roll(active, 1, 0))
    back_two = jnp.where(frame < 2, jnp.where(frame == 0, active, back_one), pltpu.roll(active, 2, 0))
    taps = convw_ref.shape[0] // 3
    shares = sum(
        dot_minor(part.astype(jnp.bfloat16), convw_ref[a * taps : (a + 1) * taps, :])
        for a, part in enumerate((back_two, back_one, active))
    )
    line = shares.shape[0] // 2
    tap = taps // 3

    def share_of(row, b):
        piece = shares[row * line : (row + 1) * line, b * tap : (b + 1) * tap]
        return jnp.concatenate([piece, jnp.zeros((line, 128 - tap), jnp.float32)], axis=1)

    zown[0] = share_of(0, 2)
    zown[1] = share_of(0, 1) + share_of(1, 2)
    zown[2] = share_of(0, 0) + share_of(1, 1)
    zown[3] = share_of(1, 0)

    def rim(src, dst, i, device):
        return remote(src, dst, h_send.at[i], h_recv.at[i], device)

    up = [rim(zown.at[0], zhigh.at[i], i, (s - 1, (h, 1 - h)[i])) for i in range(2)]
    down = [rim(zown.at[3], zlow.at[i], 2 + i, (s + 1, (h, 1 - h)[i])) for i in range(2)]
    side = rim(zown.at[pl.ds(1, 2)], zside, 4, (s, 1 - h))

    @pl.when(s > 0)
    def _():
        for copy in up:
            copy.start()

    @pl.when(s < seq_n - 1)
    def _():
        for copy in down:
            copy.start()

    side.start()

    @pl.when(s == 0)
    def _():
        zlow[...] = jnp.zeros_like(zlow)

    @pl.when(s == seq_n - 1)
    def _():
        zhigh[...] = jnp.zeros_like(zhigh)

    pair_copy.wait_recv()

    def fold_pair(xx, zz):
        return fstage[2 * zz + xx, half_rows(core), :] + fpair[2 * zz + xx]

    def fz_copy(dz):
        peer = lax.rem(z + dz, z_n)
        return remote(
            fzsend.at[peer],
            fzbuf.at[dz],
            fz_send.at[dz],
            fz_recv.at[dz],
            (peer * NEAR + lax.rem(s, NEAR), h),
        )

    for dz in range(1, z_n):
        peer = lax.rem(z + dz, z_n)
        for xx in range(2):
            fzsend[peer, xx] = fold_pair(xx, peer).astype(fzsend.dtype)
        fz_copy(dz).start()

    stat_wait(s_recv)

    def c_wait(i):
        remote(ctx_ref, cbuf.at[i], c_send.at[0], c_recv.at[i], (there, h)).wait_recv()

    @pl.when(core != h)
    def _():
        c_wait(0)

    c_wait(1)
    mod_copy.wait_recv()
    w_copy.wait_recv()
    text_sums = jnp.sum(sbuf[...], axis=0)
    sum_at = lax.broadcasted_iota(jnp.int32, (8, half), 0)
    text_sums = jnp.where(sum_at == 0, text_sums[0:1], text_sums[1:2])
    text_sums = jnp.transpose(text_sums) / width_full
    text_mean = text_sums[:, 0:1]
    text_scale = lax.rsqrt(text_sums[:, 1:2] - text_mean * text_mean + eps_norm)
    lhs = []
    for i, mods in enumerate((tmod_ref, mbuf)):
        text_normed = (cbuf[i].astype(jnp.float32) - text_mean) * text_scale
        text_normed = text_normed * (1.0 + mods[1:2, :]) + mods[0:1, :]
        lhs.append(split_high_low(text_normed))

    def text_piece(xx, zz):
        hh = 2 * zz + xx
        out = None
        for (high, low), ref in zip(lhs, (wt_ref, wbuf)):
            w = jnp.concatenate(
                [
                    ref[:, pl.ds(pl.multiple_of(i * width + hh * HD, HD), HD)]
                    for i in range(2)
                ],
                axis=1,
            )
            term = dot_f32(high, w) + dot_f32(low, w)
            out = term if out is None else out + term
        return out

    def tx_copy(i):
        peer = lax.rem(z + 1 + i, z_n)
        return remote(tstage.at[peer], txbuf.at[peer], tx_send.at[i], tx_recv.at[i], across)

    def text_out(i):
        peer = lax.rem(z + 1 + i, z_n)
        tstage[peer] = text_piece(1 - x, peer).astype(jnp.bfloat16)
        tx_copy(i).start()

    text_out(0)
    text_out(1)

    @pl.when(s < seq_n - 1)
    def _():
        for copy in up:
            copy.wait_recv()

    @pl.when(s > 0)
    def _():
        for copy in down:
            copy.wait_recv()

    side.wait_recv()
    blocks = []
    lane = lanes_of((8, 128))
    conv_bias = jnp.concatenate([convb_ref[...], jnp.zeros((1, 112), jnp.float32)], axis=1)
    for row in range(2):
        rims = zlow if row == 0 else zhigh
        mine = zown[1 + row] + rims[0]
        other = zside[row] + rims[1]
        cols = [mine[8 * i : 8 * i + 8] for i in range(line // 8)]
        left = jnp.where(h == 1, other[line - 8 : line], 0.0)
        right = jnp.where(h == 0, other[0:8], 0.0)
        cols = [left] + cols + [right]
        for i in range(line // 8):
            got = cols[i] + pltpu.roll(cols[i + 1], 128 - 16, 1) + pltpu.roll(cols[i + 2], 128 - 32, 1)
            got = jnp.where(lane < 16, got + conv_bias, 0.0)
            at = 16 * (2 * row + i % 2)
            blocks.append(got if at == 0 else pltpu.roll(got, at, 1))
    per_row = line // 8
    tokens = [
        blocks[2 * q] + blocks[2 * q + 1] + blocks[per_row + 2 * q] + blocks[per_row + 2 * q + 1]
        for q in range(per_row // 2)
    ]
    patches = jnp.concatenate(tokens, axis=0).astype(jnp.bfloat16)
    hidden = dot_f32(patches[:, : pw_ref.shape[0]], pw_ref[...]) + pb_ref[...]
    center = jnp.mean(hidden, axis=1, keepdims=True)
    offset = hidden - center
    spread_of = jnp.mean(offset * offset, axis=1, keepdims=True)
    rstd = lax.rsqrt(spread_of + eps_norm)
    hidden_ref[...] = hidden
    r_high = rstd.astype(jnp.bfloat16).astype(jnp.float32)
    r_mid = (rstd - r_high).astype(jnp.bfloat16).astype(jnp.float32)
    r_low = rstd - r_high - r_mid
    lane = lanes_of((own_rows, 128))
    block = patches.astype(jnp.float32)
    for at, value in ((64, jnp.ones_like(rstd)), (65, r_high), (66, r_mid), (67, r_low)):
        block = jnp.where(lane == at, value, block)
    psrc[...] = block.astype(jnp.bfloat16)
    pbuf[me] = psrc[...]
    p_begin()

    for i in range(2, z_n - 1):
        text_out(i)

    def tz_copy(dz):
        peer = lax.rem(z + dz, z_n)
        return remote(
            tzsend.at[peer],
            tzbuf.at[dz],
            tz_send.at[dz],
            tz_recv.at[dz],
            (peer * NEAR + lax.rem(s, NEAR), h),
        )

    def text_sum(i):
        peer = lax.rem(z + 1 + i, z_n)
        mine = text_piece(x, peer)
        tx_copy(i).wait_recv()
        return mine + txbuf[peer].astype(jnp.float32)

    def text_on(i):
        tzsend[lax.rem(z + 1 + i, z_n)] = text_sum(i).astype(jnp.bfloat16)
        tz_copy(i + 1).start()

    text_on(0)
    text_on(1)

    for dz in range(1, z_n):
        fz_copy(dz).wait_recv()

    def fold_sum(xx):
        out = fold_pair(xx, z)
        for dz in range(1, z_n):
            out = out + fzbuf[dz, xx].astype(jnp.float32)
        return out

    fxsend[...] = fold_sum(1 - x).astype(fxsend.dtype)
    fx_copy = remote(fxsend, fxbuf, m_send.at[3], m_recv.at[3], across)
    fx_copy.start()
    text_out(z_n - 1)
    wout_copy.start()
    for i in range(2, z_n - 1):
        text_on(i)

    fold_half = fold_sum(x)
    fx_copy.wait_recv()
    fold_half = fold_half + fxbuf[...].astype(jnp.float32)
    ffull[half_rows(core), :] = fold_half
    fold_copy = remote(
        ffull.at[half_rows(core), :], ffull.at[half_rows(core), :], m_send.at[4], m_recv.at[4], sibling
    )
    fold_copy.start()
    remote(
        ffull.at[half_rows(core), :], ffull.at[half_rows(1 - core), :], m_send.at[4], m_recv.at[4], sibling
    ).wait_recv()
    fold = ffull[...]
    shift = fold[68:69, :]
    row_at = lax.broadcasted_iota(jnp.int32, fold.shape, 0)
    fold_high, fold_low = split_high_low(jnp.where(row_at < 65, fold, 0.0))
    p_arrive()
    all_tokens = pbuf[...].reshape(count * own_rows, 128)
    tail = all_tokens[:, 64:].astype(jnp.float32)
    scale_of = tail[:, 1:2] + tail[:, 2:3] + tail[:, 3:4]
    tokens_in = all_tokens[:, : fold.shape[0]]
    qkv = (dot_f32(tokens_in, fold_high) + dot_f32(tokens_in, fold_low)) * scale_of + shift
    qkv = qkv.astype(jnp.bfloat16)
    qbuf[...] = qkv[:, :HD]
    pair = head_n * own_rows
    query = jnp.concatenate(
        [qbuf[pl.ds(pl.multiple_of((2 * k + core) * pair, pair), pair), :] for k in range(heads_here)],
        axis=0,
    )
    image_scores = dot_minor(query, qkv[:, HD : 2 * HD]) / HD

    text_own = text_sum(z_n - 1)
    for dz in range(1, z_n):
        tz_copy(dz).wait_recv()
    for dz in range(1, z_n):
        text_own = text_own + tzbuf[dz].astype(jnp.float32)
    tkv[core] = text_own.astype(jnp.bfloat16)
    text_copy = remote(tkv.at[core], tkv.at[core], m_send.at[5], m_recv.at[5], sibling)
    text_copy.start()
    remote(tkv.at[core], tkv.at[1 - core], m_send.at[5], m_recv.at[5], sibling).wait_recv()
    text_kv = tkv[...].reshape(-1, 2 * HD)
    text_scores = dot_minor(query, text_kv[:, :HD]) / HD
    text_scores = jnp.where(lanes_of(text_scores.shape) < len_ref[0], text_scores, -1e30)
    top = jnp.maximum(
        jnp.max(image_scores, axis=1, keepdims=True), jnp.max(text_scores, axis=1, keepdims=True)
    )
    image_probs = jnp.exp(image_scores - top)
    text_probs = jnp.exp(text_scores - top)
    totals = jnp.sum(image_probs, axis=1, keepdims=True) + jnp.sum(text_probs, axis=1, keepdims=True)
    attended = dot_f32(image_probs.astype(jnp.bfloat16), qkv[:, 2 * HD :])
    attended = attended + dot_f32(text_probs.astype(jnp.bfloat16), text_kv[:, HD:])
    attended = (attended / totals).astype(jnp.bfloat16)
    attsend[...] = attended.reshape(heads_here, pair, HD)

    def a_copy(k, owner, i):
        return remote(
            attsend.at[k],
            attrecv.at[:, pl.ds(pl.multiple_of(owner * HD, HD), HD)],
            a_send.at[i],
            a_recv.at[i],
            (2 * k + core, h),
        )

    for off in range(1, heads_here):
        a_copy(lax.rem(chip + off, heads_here), chip, off).start()
    attrecv[:, pl.ds(pl.multiple_of(chip * HD, HD), HD)] = attsend[chip]
    wout_copy.wait()
    for off in range(1, heads_here):
        a_copy(chip, lax.rem(chip + heads_here - off, heads_here), off).wait_recv()

    rows = attrecv[...]
    chunks = y_send.shape[0]
    chunk = width_full // chunks

    def y_copy(j):
        at = pl.ds(j * chunk, chunk)
        return remote(
            ysend.at[:, at], yrecv.at[:, at], y_send.at[j], y_recv.at[j], (s, 1 - h)
        )

    for j in range(chunks):
        part = dot_f32(rows, woutv[:, j * chunk : (j + 1) * chunk])
        first, second = part[:own_rows], part[own_rows:]
        ysend[:, j * chunk : (j + 1) * chunk] = jnp.where(h == 0, second, first).astype(jnp.bfloat16)
        proj[:, j * chunk : (j + 1) * chunk] = jnp.where(h == 0, first, second)
        y_copy(j).start()
    def out_copy(j):
        at = pl.ds(j * chunk, chunk)
        return pltpu.make_async_copy(out_ref.at[:, at], out_hbm.at[:, at], out_sem.at[j])

    g_sent()
    p_sent()

    stat_wait(s_send)
    far_copy.wait_send()

    @pl.when(core != h)
    def _():
        near_copy.wait_send()

    for copy in (w_copy, mod_copy, pair_copy, fx_copy, fold_copy, text_copy, side):
        copy.wait_send()

    @pl.when(s > 0)
    def _():
        for copy in up:
            copy.wait_send()

    @pl.when(s < seq_n - 1)
    def _():
        for copy in down:
            copy.wait_send()

    for dz in range(1, z_n):
        fz_copy(dz).wait_send()
        tz_copy(dz).wait_send()
    for i in range(z_n):
        tx_copy(i).wait_send()
    for off in range(1, heads_here):
        a_copy(lax.rem(chip + off, heads_here), chip, off).wait_send()
    for j in range(chunks):
        y_copy(j).wait_recv()
        at = slice(j * chunk, (j + 1) * chunk)
        projected = proj[:, at] + yrecv[:, at].astype(jnp.float32) + ob_ref[:, at]
        out_ref[:, at] = (hidden_ref[:, at] + mod_ref[2:3, at] * projected).astype(jnp.bfloat16)
        out_copy(j).start()
    for j in range(chunks):
        y_copy(j).wait_send()
        out_copy(j).wait()


def fused_body(
    features,
    gn_gain,
    gn_bias,
    conv_weight,
    conv_bias,
    patch_weight,
    patch_bias,
    image_mod,
    w_qkv,
    text_ids,
    text_length,
    text_table,
    text_mod,
    w_text,
    w_out,
    out_bias,
):
    frame_count, row_count, col_count, chan_count = features.shape
    width_full = patch_weight.shape[1]
    seq_n, head_n = lax.axis_size("seq"), lax.axis_size("head")
    depth, _, head_width = w_qkv.shape
    heads_here = head_width // HD
    z_n = seq_n // NEAR
    cells = frame_count * row_count * col_count
    own = cells // 4
    half = text_ids.shape[0] // 2
    count = seq_n * head_n
    f32, bf16 = jnp.float32, jnp.bfloat16

    anywhere = pl.BlockSpec(memory_space=pl.ANY)
    sems = pltpu.SemaphoreType.DMA
    scratch = pltpu.VMEM
    line = cells // 2
    fold_shape = (48, 3 * HD)
    out = pl.pallas_call(
        functools.partial(fused_kernel, seq_n, head_n, cells * (chan_count // GN_GROUPS) * count),
        out_shape=jax.ShapeDtypeStruct((own, width_full), bf16),
        in_specs=[anywhere, pl.BlockSpec(memory_space=pltpu.SMEM)] + [anywhere] * 14,
        out_specs=anywhere,
        scratch_shapes=[
            scratch((depth, 2 * head_width), bf16),
            scratch((own, width_full), bf16),
            scratch(features.shape, bf16),
            scratch(patch_weight.shape, bf16),
            scratch((1, width_full), f32),
            scratch(image_mod.shape, f32),
            scratch((1, text_ids.shape[0]), jnp.int32),
            scratch((1, chan_count), f32),
            scratch((1, chan_count), f32),
            scratch((27 * conv_bias.shape[0], chan_count), bf16),
            scratch((1, conv_bias.shape[0]), f32),
            scratch(text_mod.shape, f32),
            scratch((1, width_full), f32),
            scratch((cells, chan_count), f32),
            scratch((depth, text_table.shape[1]), bf16),
            scratch((3, depth, head_width), bf16),
            scratch((half, depth), bf16),
            scratch((2, half), f32),
            scratch((8, 128), f32),
            scratch((count, 8, 128), f32),
            scratch((4, line, 128), f32),
            scratch((2, line, 128), f32),
            scratch((2, line, 128), f32),
            scratch((2, line, 128), f32),
            scratch((own, 128), bf16),
            scratch((count, own, 128), bf16),
            scratch((seq_n, 2, half), f32),
            scratch((2, half, depth), bf16),
            scratch((depth, 2 * head_width), bf16),
            scratch((2, depth), f32),
            scratch((heads_here, 2 * fold_shape[0], 3 * HD), f32),
            scratch((heads_here, *fold_shape), f32),
            scratch(fold_shape, bf16),
            scratch(fold_shape, bf16),
            scratch((z_n, 2, *fold_shape), bf16),
            scratch((z_n, 2, *fold_shape), bf16),
            scratch((2 * fold_shape[0], 3 * HD), f32),
            scratch((z_n, half, 2 * HD), bf16),
            scratch((z_n, half, 2 * HD), bf16),
            scratch((z_n, half, 2 * HD), bf16),
            scratch((z_n, half, 2 * HD), bf16),
            scratch((2, half, 2 * HD), bf16),
            scratch((count * own, HD), bf16),
            scratch((heads_here, head_n * own, HD), bf16),
            scratch((head_n * own, head_width), bf16),
            scratch((own, width_full), f32),
            scratch((own, width_full), bf16),
            scratch((own, width_full), bf16),
            scratch((own, width_full), f32),
            scratch((head_width, width_full), bf16),
            sems((12,)),
            sems((4,)),
            sems((8,)),
            sems,
            sems,
            sems,
            sems,
            sems,
            sems,
            sems,
            sems,
            sems((2,)),
            sems((2,)),
            sems((6,)),
            sems((6,)),
            sems((5,)),
            sems((5,)),
            sems((z_n,)),
            sems((z_n,)),
            sems((z_n,)),
            sems((z_n,)),
            sems((z_n,)),
            sems((z_n,)),
            sems((heads_here,)),
            sems((heads_here,)),
            sems((4,)),
            sems((4,)),
        ],
        compiler_params=pltpu.CompilerParams(
            collective_id=3, has_side_effects=True, vmem_limit_bytes=60 * 1024 * 1024
        ),
    )(
        w_text.reshape(depth, 2 * head_width),
        text_length,
        features,
        patch_weight,
        patch_bias[None],
        image_mod,
        text_ids[None],
        gn_gain[None],
        gn_bias[None],
        conv_weight.reshape(-1, chan_count),
        conv_bias[None],
        text_mod,
        out_bias[None],
        text_table,
        w_qkv.transpose(1, 0, 2),
        w_out,
    )
    out = out.reshape(col_count // 2, frame_count, width_full).transpose(1, 0, 2)
    return out.reshape(frame_count, row_count // 2, col_count // 2, width_full)


def choose_body(*operands):
    features, w_qkv = operands[0], operands[8]
    seq_n, head_n = lax.axis_size("seq"), lax.axis_size("head")
    pair = seq_n == 2 * (w_qkv.shape[2] // HD) and head_n == 2 and seq_n % NEAR == 0
    small = features.shape[:3] == (8, 2, 4) and features.shape[3] == 512
    return fused_body(*operands) if pair and small else body(*operands)


def solution(mesh):
    return jax.shard_map(
        choose_body,
        mesh=mesh,
        in_specs=(
            P(None, "seq", "head", None),
            P(),
            P(),
            P(),
            P(),
            P(),
            P(),
            P(),
            P("seq", None, "head"),
            P(),
            P(),
            P("seq", None),
            P(None, "seq"),
            P("seq", None, "head"),
            P("head", None),
            P(),
        ),
        out_specs=P(None, "seq", "head", None),
        check_vma=False,
    )
```

```python
import functools

import jax
import jax.numpy as jnp
from jax import lax
from jax.experimental import pallas as pl
from jax.experimental.pallas import tpu as pltpu
from jax.sharding import PartitionSpec as P

HD = 128
GN_GROUPS = 32
CHUNK = 512

eps_norm = 1e-06


MESH = pl.DeviceIdType.MESH


def place_of(index, head_n):
    return (lax.div(index, head_n), lax.rem(index, head_n))


def greet_all(seq_n, head_n):
    count = seq_n * head_n
    me = lax.axis_index("seq") * head_n + lax.axis_index("head")
    barrier = pltpu.get_barrier_semaphore()

    def greet(off, carry):
        pl.semaphore_signal(
            barrier,
            inc=1,
            device_id=place_of(lax.rem(me + off, count), head_n),
            device_id_type=MESH,
        )
        return carry

    lax.fori_loop(1, count, greet, 0)
    pl.semaphore_wait(barrier, count - 1)


def start_share(seq_n, head_n, x_ref, out_ref, local_sem, send_sem, recv_sem):
    count = seq_n * head_n
    me = lax.axis_index("seq") * head_n + lax.axis_index("head")

    def copy(off, slot):
        return pltpu.make_async_remote_copy(
            src_ref=x_ref,
            dst_ref=out_ref.at[slot],
            send_sem=send_sem.at[off],
            recv_sem=recv_sem.at[off],
            device_id=place_of(lax.rem(me + off, count), head_n),
            device_id_type=MESH,
        )

    def send(off, carry):
        copy(off, me).start()
        return carry

    lax.fori_loop(1, count, send, 0)
    own = pltpu.make_async_copy(x_ref, out_ref.at[me], local_sem)
    own.start()

    def finish():
        own.wait()

        def wait(off, carry):
            copy(off, me).wait_send()
            copy(off, lax.rem(me + count - off, count)).wait_recv()
            return carry

        lax.fori_loop(1, count, wait, 0)

    return finish


def share_kernel(seq_n, head_n, x_ref, out_ref, local_sem, send_sem, recv_sem):
    greet_all(seq_n, head_n)
    start_share(seq_n, head_n, x_ref, out_ref, local_sem, send_sem, recv_sem)()


def swap_kernel(seq_n, x_ref, out_ref, local_sem, send_sem, recv_sem):
    me, h = lax.axis_index("seq"), lax.axis_index("head")
    barrier = pltpu.get_barrier_semaphore()

    def greet(off, carry):
        pl.semaphore_signal(
            barrier, inc=1, device_id=(lax.rem(me + off, seq_n), h), device_id_type=MESH
        )
        return carry

    lax.fori_loop(1, seq_n, greet, 0)
    pl.semaphore_wait(barrier, seq_n - 1)

    def copy(off, slot):
        peer = lax.rem(me + off, seq_n)
        return pltpu.make_async_remote_copy(
            src_ref=x_ref.at[peer],
            dst_ref=out_ref.at[slot],
            send_sem=send_sem.at[off],
            recv_sem=recv_sem.at[off],
            device_id=(peer, h),
            device_id_type=MESH,
        )

    def send(off, carry):
        copy(off, me).start()
        return carry

    lax.fori_loop(1, seq_n, send, 0)
    own = pltpu.make_async_copy(x_ref.at[me], out_ref.at[me], local_sem)
    own.start()
    own.wait()

    def wait(off, carry):
        copy(off, me).wait_send()
        copy(off, lax.rem(me + seq_n - off, seq_n)).wait_recv()
        return carry

    lax.fori_loop(1, seq_n, wait, 0)


def swap(x):
    seq_n = lax.axis_size("seq")
    return pl.pallas_call(
        functools.partial(swap_kernel, seq_n),
        out_shape=jax.ShapeDtypeStruct(x.shape, x.dtype),
        in_specs=[pl.BlockSpec(memory_space=pltpu.VMEM)],
        out_specs=pl.BlockSpec(memory_space=pltpu.VMEM),
        scratch_shapes=[
            pltpu.SemaphoreType.DMA,
            pltpu.SemaphoreType.DMA((seq_n,)),
            pltpu.SemaphoreType.DMA((seq_n,)),
        ],
        compiler_params=pltpu.CompilerParams(collective_id=1, has_side_effects=True),
    )(x)


def share(x, collective_id):
    seq_n, head_n = lax.axis_size("seq"), lax.axis_size("head")
    count = seq_n * head_n
    return pl.pallas_call(
        functools.partial(share_kernel, seq_n, head_n),
        out_shape=jax.ShapeDtypeStruct((count, *x.shape), x.dtype),
        in_specs=[pl.BlockSpec(memory_space=pltpu.VMEM)],
        out_specs=pl.BlockSpec(memory_space=pltpu.VMEM),
        scratch_shapes=[
            pltpu.SemaphoreType.DMA,
            pltpu.SemaphoreType.DMA((count,)),
            pltpu.SemaphoreType.DMA((count,)),
        ],
        compiler_params=pltpu.CompilerParams(collective_id=collective_id, has_side_effects=True),
    )(x)


def weights_kernel(
    heads_here,
    group,
    wq_ref,
    wt_ref,
    ctx_ref,
    x_ref,
    w_ref,
    full_ref,
    parts_ref,
    local_sem,
    send_sem,
    recv_sem,
    pass_send,
    pass_recv,
    share_local,
    share_send,
    share_recv,
):
    s, h = lax.axis_index("seq"), lax.axis_index("head")
    mine, place = lax.div(s, group), lax.rem(s, group)
    width = heads_here * HD
    greet_all(lax.axis_size("seq"), lax.axis_size("head"))
    finish_share = start_share(
        lax.axis_size("seq"), lax.axis_size("head"), x_ref, parts_ref, share_local, share_send, share_recv
    )

    def pieces(head, slot):
        out = []
        for i in range(5):
            ref, at = (wq_ref, i) if i < 3 else (wt_ref, i - 3)
            start = pl.multiple_of(at * width + head * HD, HD)
            out.append((ref.at[:, pl.ds(start, HD)], w_ref.at[slot, :, pl.ds(i * HD, HD)]))
        out.append((ctx_ref, full_ref.at[slot]))
        return out

    def first(off, slot):
        head = lax.rem(mine + off, heads_here)
        return [
            pltpu.make_async_remote_copy(
                src_ref=src,
                dst_ref=dst,
                send_sem=send_sem.at[off, i],
                recv_sem=recv_sem.at[off, i],
                device_id=(head * group + place, h),
                device_id_type=MESH,
            )
            for i, (src, dst) in enumerate(pieces(head, slot))
        ]

    def second(off, piece, slot):
        peer = mine * group + lax.rem(place + off, group)
        return [
            pltpu.make_async_remote_copy(
                src_ref=ref.at[slot],
                dst_ref=ref.at[slot],
                send_sem=pass_send.at[off, piece, i],
                recv_sem=pass_recv.at[off, piece, i],
                device_id=(peer, h),
                device_id_type=MESH,
            )
            for i, ref in enumerate((w_ref, full_ref))
        ]

    for off in range(1, heads_here):
        for copy in first(off, s):
            copy.start()
    own = [
        pltpu.make_async_copy(src, dst, local_sem.at[i])
        for i, (src, dst) in enumerate(pieces(mine, s))
    ]
    for copy in own:
        copy.start()
    for copy in own:
        copy.wait()
    for piece in range(heads_here):
        slot = lax.rem(mine + heads_here - piece, heads_here) * group + place
        if piece > 0:
            for copy in first(piece, slot):
                copy.wait_recv()
        for off in range(1, group):
            for copy in second(off, piece, slot):
                copy.start()
    for off in range(1, heads_here):
        for copy in first(off, s):
            copy.wait_send()
    for piece in range(heads_here):
        from_group = lax.rem(mine + heads_here - piece, heads_here) * group
        for off in range(1, group):
            for copy in second(off, piece, from_group + place):
                copy.wait_send()
            for copy in second(off, piece, from_group + lax.rem(place + group - off, group)):
                copy.wait_recv()
    finish_share()


def gather_weights(w_qkv, w_text, own_context, shares):
    seq_n = lax.axis_size("seq")
    depth, _, head_width = w_qkv.shape
    heads_here = head_width // HD
    group = seq_n // heads_here
    count = seq_n * lax.axis_size("head")
    text_count = own_context.shape[1]
    anywhere = pl.BlockSpec(memory_space=pl.ANY)
    sems = pltpu.SemaphoreType.DMA
    return pl.pallas_call(
        functools.partial(weights_kernel, heads_here, group),
        out_shape=(
            jax.ShapeDtypeStruct((seq_n, depth, 5 * HD), w_qkv.dtype),
            jax.ShapeDtypeStruct((seq_n, depth, text_count), own_context.dtype),
            jax.ShapeDtypeStruct((count, *shares.shape), shares.dtype),
        ),
        in_specs=[anywhere] * 3 + [pl.BlockSpec(memory_space=pltpu.VMEM)],
        out_specs=(anywhere, anywhere, pl.BlockSpec(memory_space=pltpu.VMEM)),
        scratch_shapes=[
            sems((6,)),
            sems((heads_here, 6)),
            sems((heads_here, 6)),
            sems((group, heads_here, 2)),
            sems((group, heads_here, 2)),
            sems,
            sems((count,)),
            sems((count,)),
        ],
        compiler_params=pltpu.CompilerParams(collective_id=2, has_side_effects=True),
    )(w_qkv.reshape(depth, 3 * head_width), w_text.reshape(depth, 2 * head_width), own_context, shares)


def group_norm(features, gn_gain, gn_bias, text_mod):
    frame_count, row_count, col_count, chan_count = features.shape
    per_group = chan_count // GN_GROUPS
    values = features.astype(jnp.float32)
    chan_sums = jnp.stack(
        [jnp.sum(values, axis=(0, 1, 2)), jnp.sum(values * values, axis=(0, 1, 2))]
    )
    sums = jnp.sum(chan_sums.reshape(2, GN_GROUPS, per_group), axis=2)
    seq_n, head_n = lax.axis_size("seq"), lax.axis_size("head")
    depth = text_mod.shape[1]
    lines = -(-depth // 128)
    mod = jnp.pad(text_mod, ((0, 0), (0, lines * 128 - depth))).reshape(2 * lines, 128)
    block = jnp.concatenate([jnp.pad(sums, ((0, 0), (0, 128 - GN_GROUPS))), mod], axis=0)
    block = jnp.pad(block, ((0, -block.shape[0] % 8), (0, 0)))
    shared = share(block, 0)
    sums = jnp.sum(shared[:, :2, :GN_GROUPS], axis=0)
    mod = shared.reshape(seq_n, head_n, -1, 128)[:, 0, 2 : 2 + 2 * lines]
    mod = mod.reshape(seq_n, 2, lines * 128)[:, :, :depth]
    mod = mod.transpose(1, 0, 2).reshape(2, seq_n * depth)
    cell_count = (
        frame_count * row_count * col_count * per_group * lax.axis_size("seq") * lax.axis_size("head")
    )
    mean = sums[0] / cell_count
    scale = lax.rsqrt(sums[1] / cell_count - mean * mean + eps_norm)
    mean = jnp.repeat(mean, per_group)
    scale = jnp.repeat(scale, per_group)
    normed = (values - mean) * scale
    return jax.nn.silu(normed * gn_gain + gn_bias).astype(jnp.bfloat16), mod


def join_rims(parts, block_dim, dim, unit):
    size = parts.shape[dim]
    blocks = parts.shape[block_dim]
    core = lax.slice_in_dim(parts, unit, size - unit, axis=dim)
    low = lax.slice_in_dim(parts, 0, unit, axis=dim)
    high = lax.slice_in_dim(parts, size - unit, size, axis=dim)
    low = lax.slice_in_dim(low, 1, blocks, axis=block_dim)
    high = lax.slice_in_dim(high, 0, blocks - 1, axis=block_dim)
    pad_low = [(0, 0)] * parts.ndim
    pad_low[block_dim] = (0, 1)
    pad_low[dim] = (size - 3 * unit, 0)
    pad_high = [(0, 0)] * parts.ndim
    pad_high[block_dim] = (1, 0)
    pad_high[dim] = (0, size - 3 * unit)
    return core + jnp.pad(low, pad_low) + jnp.pad(high, pad_high)


def conv_shares(activated, conv_weight):
    padded = jnp.concatenate([activated[:1], activated[:1], activated], axis=0)
    shares = lax.conv_general_dilated(
        padded[None],
        conv_weight,
        (1, 1, 1),
        ((0, 0), (2, 2), (2, 2)),
        dimension_numbers=("NDHWC", "DHWOI", "NDHWC"),
        preferred_element_type=jnp.float32,
    )[0]
    return shares.reshape(-1, 128)


def all_patches(parts, frame_count, row_count, col_count, conv_bias):
    seq_n, head_n = lax.axis_size("seq"), lax.axis_size("head")
    chans = conv_bias.shape[0]
    parts = parts.reshape(
        seq_n, head_n, frame_count, row_count + 2, (col_count + 2) * chans
    )
    parts = join_rims(join_rims(parts, 0, 3, 1), 1, 4, chans)
    latent = (parts + jnp.tile(conv_bias, col_count)).astype(jnp.bfloat16)
    blocks = latent.reshape(
        seq_n, head_n, frame_count, row_count // 2, 2, col_count // 2, 2 * chans
    )
    blocks = blocks.transpose(0, 1, 2, 3, 5, 4, 6)
    own = frame_count * (row_count // 2) * (col_count // 2)
    return blocks.reshape(seq_n * head_n * own, 4 * chans)


def modulate(patches, patch_weight, patch_bias, image_mod):
    hidden = jnp.dot(patches, patch_weight, preferred_element_type=jnp.float32) + patch_bias
    center = jnp.mean(hidden, axis=1, keepdims=True)
    offset = hidden - center
    spread = jnp.mean(offset * offset, axis=1, keepdims=True)
    normed = offset * lax.rsqrt(spread + eps_norm)
    return (normed * (1.0 + image_mod[1]) + image_mod[0]).astype(jnp.bfloat16)


def body(
    features,
    gn_gain,
    gn_bias,
    conv_weight,
    conv_bias,
    patch_weight,
    patch_bias,
    image_mod,
    w_qkv,
    text_ids,
    text_length,
    text_table,
    text_mod,
    w_text,
    w_out,
    out_bias,
):
    frame_count, row_count, col_count, _ = features.shape
    width_full = patch_weight.shape[1]
    seq_n, head_n = lax.axis_size("seq"), lax.axis_size("head")
    seq_i, head_i = lax.axis_index("seq"), lax.axis_index("head")
    depth, _, head_width = w_qkv.shape
    heads_here = head_width // HD
    group = seq_n // heads_here
    text_count = text_ids.shape[0]

    chosen = (
        lax.broadcasted_iota(jnp.int32, (text_table.shape[1], text_count), 0) == text_ids[None, :]
    ).astype(jnp.bfloat16)
    own_context = jnp.dot(text_table, chosen, preferred_element_type=jnp.float32).astype(
        jnp.bfloat16
    )
    activated, mod = group_norm(features, gn_gain, gn_bias, text_mod)
    shares = conv_shares(activated, conv_weight)
    weights, context, parts = gather_weights(w_qkv, w_text, own_context, shares)
    weights = weights.reshape(width_full, 5 * HD)
    context = context.reshape(width_full, text_count).astype(jnp.float32)
    text_mean = jnp.sum(context, axis=0) / width_full
    text_square = jnp.sum(context * context, axis=0) / width_full
    text_scale = lax.rsqrt(text_square - text_mean * text_mean + eps_norm)
    text_normed = (context - text_mean) * text_scale * (1.0 + mod[1][:, None]) + mod[0][:, None]
    text_high = text_normed.astype(jnp.bfloat16)
    text_low = (text_normed - text_high.astype(jnp.float32)).astype(jnp.bfloat16)
    w_text_flat = weights[:, 3 * HD :]
    text_kv = sum(
        lax.dot_general(
            part, w_text_flat, (((0,), (0,)), ((), ())), preferred_element_type=jnp.float32
        )
        for part in (text_high, text_low)
    ).astype(jnp.bfloat16)

    patches = all_patches(parts, frame_count, row_count, col_count, conv_bias)
    own = patches.shape[0] // (seq_n * head_n)
    part_rows = head_n * own // group
    my_part = seq_i % group
    chunk = min(CHUNK, patches.shape[0])

    def project(rows):
        modulated = modulate(rows, patch_weight, patch_bias, image_mod)
        qkv = jnp.dot(modulated, weights[:, : 3 * HD], preferred_element_type=jnp.float32)
        query, kv = qkv[:, :HD], qkv[:, HD:]
        query = lax.dynamic_index_in_dim(
            query.reshape(-1, group, part_rows, HD), my_part, axis=1, keepdims=False
        )
        return kv.astype(jnp.bfloat16), query.reshape(-1, HD).astype(jnp.bfloat16)

    if chunk == patches.shape[0]:
        image_kv, query = project(patches)
    else:
        image_kv, query = lax.map(project, patches.reshape(-1, chunk, patches.shape[1]))
        image_kv = image_kv.reshape(-1, 2 * HD)
        query = query.reshape(-1, HD)

    keys = jnp.concatenate([image_kv[:, :HD], text_kv[:, :HD]], axis=0)
    vals = jnp.concatenate([image_kv[:, HD:], text_kv[:, HD:]], axis=0)
    key_valid = (
        jnp.arange(keys.shape[0], dtype=jnp.int32) < image_kv.shape[0] + text_length[0]
    )
    scores = (
        lax.dot_general(query, keys, (((1,), (1,)), ((), ())), preferred_element_type=jnp.float32)
        / HD
    )
    scores = jnp.where(key_valid[None, :], scores, -1e30)
    probs = jnp.exp(scores - jnp.max(scores, axis=1, keepdims=True))
    totals = jnp.sum(probs, axis=1, keepdims=True)
    attended = (
        jnp.dot(probs.astype(jnp.bfloat16), vals, preferred_element_type=jnp.float32) / totals
    ).astype(jnp.bfloat16)

    attended = attended.reshape(seq_n, part_rows, HD)
    attended = swap(attended)
    attended = attended.reshape(heads_here, group, part_rows, HD).transpose(1, 2, 0, 3)
    attended = attended.reshape(head_n * own, head_width)
    if head_n == 2:
        halves = jnp.dot(attended, w_out, preferred_element_type=jnp.float32)
        halves = halves.reshape(2, own, width_full)
        away = lax.dynamic_index_in_dim(halves, 1 - head_i, 0, keepdims=False)
        here = lax.dynamic_index_in_dim(halves, head_i, 0, keepdims=False)
        projected = here + lax.ppermute(away, "head", [(0, 1), (1, 0)]) + out_bias
    else:
        projected = (
            lax.psum_scatter(
                jnp.dot(attended, w_out, preferred_element_type=jnp.float32),
                "head",
                scatter_dimension=0,
                tiled=True,
            )
            + out_bias
        )
    own_patches = lax.dynamic_slice_in_dim(patches, (seq_i * head_n + head_i) * own, own, axis=0)
    hidden = jnp.dot(own_patches, patch_weight, preferred_element_type=jnp.float32) + patch_bias
    block_out = (hidden + image_mod[2] * projected).astype(jnp.bfloat16)
    return block_out.reshape(frame_count, row_count // 2, col_count // 2, width_full)


NEAR = 4


def lanes_of(shape):
    return lax.broadcasted_iota(jnp.int32, shape, len(shape) - 1)


def group_sum(values, per_group):
    lane = lanes_of(values.shape)
    width = values.shape[-1]
    step = 1
    while step < per_group:
        above = pltpu.roll(values, width - step, 1)
        below = pltpu.roll(values, step, 1)
        values = values + jnp.where(lax.rem(lax.div(lane, step), 2) == 0, above, below)
        step *= 2
    return values


def split_high_low(values):
    high = values.astype(jnp.bfloat16)
    return high, (values - high.astype(jnp.float32)).astype(jnp.bfloat16)


def dot_f32(a, b):
    return jnp.dot(a, b, preferred_element_type=jnp.float32)


def dot_minor(a, b):
    return lax.dot_general(a, b, (((1,), (1,)), ((), ())), preferred_element_type=jnp.float32)


def fused_kernel(
    seq_n,
    head_n,
    cell_count,
    wt_hbm,
    len_ref,
    x_hbm,
    pw_hbm,
    pb_hbm,
    mod_hbm,
    ids_hbm,
    gain_hbm,
    bias_hbm,
    convw_hbm,
    convb_hbm,
    tmod_hbm,
    ob_hbm,
    table_ref,
    wq_ref,
    wout_ref,
    out_hbm,
    wt_ref,
    out_ref,
    x_raw,
    pw_ref,
    pb_ref,
    mod_ref,
    ids_ref,
    gain_ref,
    bias_ref,
    convw_ref,
    convb_ref,
    tmod_ref,
    ob_ref,
    spots,
    tablev,
    wqv,
    ctx_ref,
    stat_ref,
    gsrc,
    gbuf,
    zown,
    zlow,
    zhigh,
    zside,
    psrc,
    pbuf,
    sbuf,
    coef,
    kbuf,
    cbuf,
    wbuf,
    mbuf,
    lhs_ref,
    fstage,
    fpair,
    fxsend,
    fxbuf,
    fzsend,
    fzbuf,
    ffull,
    tstage,
    txbuf,
    tzsend,
    tzbuf,
    tkv,
    ikv,
    attsend,
    attrecv,
    proj,
    ysend,
    yrecv,
    hidden_ref,
    woutv,
    in_sem,
    out_sem,
    table_sem,
    wq_sem,
    wout_sem,
    g_send,
    g_recv,
    p_send,
    p_recv,
    s_send,
    s_recv,
    k_send,
    k_recv,
    c_send,
    c_recv,
    m_send,
    m_recv,
    h_send,
    h_recv,
    fz_send,
    fz_recv,
    tx_send,
    tx_recv,
    tz_send,
    tz_recv,
    a_send,
    a_recv,
    y_send,
    y_recv,
):
    count = seq_n * head_n
    s, h = lax.axis_index("seq"), lax.axis_index("head")
    me = s * head_n + h
    core = lax.rem(s, 2)
    x = lax.rem(lax.div(s, 2), 2)
    z = lax.div(s, NEAR)
    z_n = seq_n // NEAR
    chip = lax.div(s, 2)
    heads_here = seq_n // 2
    sibling = (s + 1 - 2 * core, h)
    across = (s + 2 - 4 * x, h)
    depth = wt_ref.shape[0]
    width = heads_here * HD
    width_full = pw_ref.shape[1]
    own_rows = psrc.shape[0]

    def remote(src, dst, send, recv, device):
        return pltpu.make_async_remote_copy(
            src_ref=src, dst_ref=dst, send_sem=send, recv_sem=recv, device_id=device, device_id_type=MESH
        )

    pieces = table_sem.shape[0]
    piece = table_ref.shape[1] // pieces

    def table_copy(i):
        at = pl.ds(i * piece, piece)
        return pltpu.make_async_copy(table_ref.at[:, at], tablev.at[:, at], table_sem.at[i])

    wq_copy = pltpu.make_async_copy(wq_ref, wqv, wq_sem)
    wout_copy = pltpu.make_async_copy(wout_ref, woutv, wout_sem)
    small = [
        pltpu.make_async_copy(src, dst, in_sem.at[i])
        for i, (src, dst) in enumerate(
            (
                (x_hbm, x_raw),
                (pw_hbm, pw_ref),
                (pb_hbm, pb_ref),
                (mod_hbm, mod_ref),
                (ids_hbm, ids_ref),
                (gain_hbm, gain_ref),
                (bias_hbm, bias_ref),
                (convw_hbm, convw_ref),
                (convb_hbm, convb_ref),
                (tmod_hbm, tmod_ref),
                (ob_hbm, ob_ref),
                (wt_hbm, wt_ref),
            )
        )
    ]
    barrier = pltpu.get_barrier_semaphore()

    def greet(off, carry):
        pl.semaphore_signal(
            barrier, inc=1, device_id=place_of(lax.rem(me + off, count), head_n), device_id_type=MESH
        )
        return carry

    small[0].start()
    lax.fori_loop(1, count, greet, 0)

    for copy in small[1:4]:
        copy.start()
    wq_copy.start()
    small[4].start()
    for i in range(2):
        table_copy(i).start()

    frames, row_n, col_n, _ = x_raw.shape
    cells = frames * row_n * col_n
    small[0].wait()
    for i in range(2, pieces):
        table_copy(i).start()
    for copy in small[5:]:
        copy.start()
    for f in range(frames):
        for r in range(row_n):
            at = (f * row_n + r) * col_n
            spots[at : at + col_n, :] = x_raw[f, r].astype(jnp.float32)
    to_at = lax.broadcasted_iota(jnp.int32, (cells, cells), 0)
    from_at = lax.broadcasted_iota(jnp.int32, (cells, cells), 1)
    wanted = lax.rem(to_at, frames) * (row_n * col_n) + lax.div(to_at, frames)
    values = dot_f32((from_at == wanted).astype(jnp.bfloat16), spots[...].astype(jnp.bfloat16))
    chan_count = values.shape[1]
    lines = chan_count // 128
    per_group = chan_count // GN_GROUPS
    total = jnp.sum(values, axis=0, keepdims=True)
    square = jnp.sum(values * values, axis=0, keepdims=True)
    for j in range(lines):
        gsrc[j : j + 1, :] = total[:, j * 128 : (j + 1) * 128]
        gsrc[lines + j : lines + j + 1, :] = square[:, j * 128 : (j + 1) * 128]
    gbuf[me] = gsrc[...]

    pl.semaphore_wait(barrier, count - 1)

    def wait_bytes(refs, sem):
        pltpu.make_async_copy(refs, refs, sem).wait()

    def spread(src, buf, send, recv):
        def begin():
            def one(off, carry):
                remote(
                    src, buf.at[me], send, recv, place_of(lax.rem(me + off, count), head_n)
                ).start()
                return carry

            lax.fori_loop(1, count, one, 0)

        def all_of(sem):
            wait_bytes(buf.at[pl.ds(0, count - 1)], sem)

        return begin, lambda: all_of(recv), lambda: all_of(send)

    g_begin, g_arrive, g_sent = spread(gsrc, gbuf, g_send, g_recv)
    same_n = count // 2
    my_same = chip * head_n + h

    def p_begin():
        def one(off, carry):
            to_chip, to_h = place_of(lax.rem(my_same + off, same_n), head_n)
            remote(psrc, pbuf.at[my_same], p_send, p_recv, (2 * to_chip + core, to_h)).start()
            return carry

        lax.fori_loop(1, same_n, one, 0)

    def p_arrive():
        wait_bytes(pbuf.at[pl.ds(0, same_n - 1)], p_recv)

    def p_sent():
        wait_bytes(pbuf.at[pl.ds(0, same_n - 1)], p_send)

    g_begin()

    w_copy = remote(wt_hbm, wbuf, m_send.at[0], m_recv.at[0], sibling)
    w_copy.start()

    def own_features(ref, rows):
        both = ref[rows, pl.ds(pl.multiple_of(chip * 2 * depth, 128), 2 * depth)].astype(jnp.float32)
        return jnp.where(core == 0, both[:, :depth], both[:, depth:])

    def feature_mean(ref):
        return jnp.mean(ref[...].astype(jnp.float32), axis=1, keepdims=True)

    for copy in small[1:4]:
        copy.wait()
    gain = 1.0 + own_features(mod_ref, slice(1, 2))
    lines_main = (own_features(pw_ref, slice(None)) - feature_mean(pw_ref)) * gain
    line_bias = (own_features(pb_ref, slice(None)) - feature_mean(pb_ref)) * gain
    line_at = lax.broadcasted_iota(jnp.int32, (16, depth), 0)
    lines_rest = jnp.where(
        line_at == 0, line_bias, jnp.where(line_at == 4, own_features(mod_ref, slice(0, 1)), 0.0)
    )
    lines_all = jnp.concatenate([lines_main, lines_rest, jnp.zeros((16, depth), jnp.float32)], axis=0)
    fold_lhs = jnp.concatenate(split_high_low(lines_all), axis=0)
    fold_rows = fstage.shape[1]
    wq_copy.wait()
    for i in range(3):
        product = dot_f32(fold_lhs, wqv[i])
        product = product[:fold_rows] + product[fold_rows:]
        for hh in range(heads_here):
            fstage[hh, :, i * HD : (i + 1) * HD] = product[:, hh * HD : (hh + 1) * HD]

    rows_half = fpair.shape[1]

    def half_rows(which):
        return pl.ds(pl.multiple_of(which * rows_half, 8), rows_half)

    pair_copy = remote(fstage.at[:, half_rows(1 - core), :], fpair, m_send.at[2], m_recv.at[2], sibling)
    pair_copy.start()

    half = ctx_ref.shape[1]
    small[4].wait()
    ids = ids_ref[:, pl.ds(pl.multiple_of(h * half, 128), half)]
    spot = lax.broadcasted_iota(jnp.int32, (piece, half), 0)

    def look_up(i, found):
        table_copy(i).wait()
        chosen = (spot == ids - i * piece).astype(jnp.bfloat16)
        return found + dot_f32(tablev[:, i * piece : (i + 1) * piece], chosen)

    found = jnp.zeros((depth, half), jnp.float32)
    for i in range(pieces // 2):
        found = look_up(i, found)

    pair_copy.wait_recv()

    def fold_pair(xx, zz):
        return fstage[2 * zz + xx, half_rows(core), :] + fpair[2 * zz + xx]

    for zz in range(z_n):
        fxsend[zz] = fold_pair(1 - x, zz).astype(fxsend.dtype)
    fx_copy = remote(fxsend, fxbuf, m_send.at[3], m_recv.at[3], across)
    fx_copy.start()

    for i in range(pieces // 2, pieces):
        found = look_up(i, found)
    stat_ref[0:1, :] = jnp.sum(found, axis=0, keepdims=True)
    stat_ref[1:2, :] = jnp.sum(found * found, axis=0, keepdims=True)
    ctx_ref[...] = found.astype(jnp.bfloat16)

    same = core == h
    slot = jnp.where(same, 0, 1)
    there = 2 * chip + h
    near_copy = remote(ctx_ref, cbuf.at[slot], c_send.at[0], c_recv.at[slot], (there, h))
    far_copy = remote(ctx_ref, cbuf.at[slot], c_send.at[1], c_recv.at[slot], (there, 1 - h))
    far_copy.start()

    @pl.when(core != h)
    def _():
        near_copy.start()

    def stat_go(j, carry):
        to_s, to_h = 2 * lax.div(j, head_n) + h, lax.rem(j, head_n)

        @pl.when((to_s != s) | (to_h != h))
        def _():
            remote(stat_ref, sbuf.at[s], s_send, s_recv, (to_s, to_h)).start()

        return carry

    def stat_wait(sem):
        @pl.when(core == h)
        def _():
            wait_bytes(sbuf.at[pl.ds(0, seq_n - 1)], sem)

        @pl.when(core != h)
        def _():
            wait_bytes(sbuf.at[pl.ds(0, seq_n)], sem)

    lax.fori_loop(0, seq_n, stat_go, 0)

    @pl.when(core == h)
    def _():
        cbuf[0] = ctx_ref[...]
        sbuf[s] = stat_ref[...]

    mod_copy = remote(tmod_ref, mbuf, m_send.at[1], m_recv.at[1], sibling)
    for copy in small[5:]:
        copy.wait()
    mod_copy.start()

    def weight_of(ref, hh):
        return jnp.concatenate(
            [ref[:, pl.ds(pl.multiple_of(i * width + hh * HD, HD), HD)] for i in range(2)], axis=1
        )

    def c_wait(i):
        remote(ctx_ref, cbuf.at[i], c_send.at[0], c_recv.at[i], (there, h)).wait_recv()

    def text_piece(xx, zz):
        hh = 2 * zz + xx
        out = None
        for i, ref in enumerate((wt_ref, wbuf)):
            w = weight_of(ref, hh)
            term = dot_f32(lhs_ref[2 * i], w) + dot_f32(lhs_ref[2 * i + 1], w)
            out = term if out is None else out + term
        return out

    ways = [z_n // 2] + [dz for dz in range(1, z_n) if dz != z_n // 2] + [0]

    def peer_of(i):
        return lax.rem(z + ways[i], z_n)

    def tx_copy(i):
        peer = peer_of(i)
        return remote(tstage.at[peer], txbuf.at[peer], tx_send, tx_recv.at[i], across)

    def text_out(i):
        peer = peer_of(i)
        tstage[peer] = text_piece(1 - x, peer).astype(jnp.bfloat16)
        tx_copy(i).start()

    def text_begin():
        mod_copy.wait_recv()
        w_copy.wait_recv()
        for i, mods in enumerate((tmod_ref, mbuf)):
            tokens_here = jnp.transpose(cbuf[i].astype(jnp.float32))
            tokens_here = tokens_here - jnp.mean(tokens_here, axis=1, keepdims=True)
            high, low = split_high_low(tokens_here * (1.0 + mods[1:2, :]))
            lhs_ref[2 * i] = high
            lhs_ref[2 * i + 1] = low
        for i in range(z_n):
            text_out(i)

    g_arrive()
    sums = group_sum(jnp.sum(gbuf[...], axis=0), per_group) / cell_count
    mean = sums[:lines]
    scale = lax.rsqrt(sums[lines:] - mean * mean + eps_norm)
    mean = jnp.concatenate([mean[j : j + 1] for j in range(lines)], axis=1)
    scale = jnp.concatenate([scale[j : j + 1] for j in range(lines)], axis=1)
    normed = (values - mean) * scale * gain_ref[...] + bias_ref[...]
    active = normed / (1.0 + jnp.exp(-normed))
    frame = lax.rem(lax.broadcasted_iota(jnp.int32, active.shape, 0), frames)
    back_one = jnp.where(frame == 0, active, pltpu.roll(active, 1, 0))
    back_two = jnp.where(frame < 2, jnp.where(frame == 0, active, back_one), pltpu.roll(active, 2, 0))
    taps = convw_ref.shape[0] // 3
    shares = sum(
        dot_minor(part.astype(jnp.bfloat16), convw_ref[a * taps : (a + 1) * taps, :])
        for a, part in enumerate((back_two, back_one, active))
    )
    line = shares.shape[0] // 2
    tap = taps // 3

    def share_of(row, b):
        piece = shares[row * line : (row + 1) * line, b * tap : (b + 1) * tap]
        return jnp.concatenate([piece, jnp.zeros((line, 128 - tap), jnp.float32)], axis=1)

    zown[0] = share_of(0, 2)
    zown[1] = share_of(0, 1) + share_of(1, 2)
    zown[2] = share_of(0, 0) + share_of(1, 1)
    zown[3] = share_of(1, 0)

    def rim(src, dst, i, device):
        return remote(src, dst, h_send.at[i], h_recv.at[i], device)

    up = [rim(zown.at[0], zhigh.at[i], i, (s - 1, (h, 1 - h)[i])) for i in range(2)]
    down = [rim(zown.at[3], zlow.at[i], 2 + i, (s + 1, (h, 1 - h)[i])) for i in range(2)]
    side = rim(zown.at[pl.ds(1, 2)], zside, 4, (s, 1 - h))

    @pl.when(s > 0)
    def _():
        for copy in up:
            copy.start()

    @pl.when(s < seq_n - 1)
    def _():
        for copy in down:
            copy.start()

    side.start()

    @pl.when(s == 0)
    def _():
        zlow[...] = jnp.zeros_like(zlow)

    @pl.when(s == seq_n - 1)
    def _():
        zhigh[...] = jnp.zeros_like(zhigh)

    fx_copy.wait_recv()

    def fold_sum(zz):
        return fold_pair(x, zz) + fxbuf[zz].astype(jnp.float32)

    for dz in range(1, z_n):
        peer = lax.rem(z + dz, z_n)
        fzsend[peer] = fold_sum(peer).astype(fzsend.dtype)
        remote(
            fzsend.at[peer],
            fzbuf.at[dz],
            fz_send,
            fz_recv,
            (peer * NEAR + lax.rem(s, NEAR), h),
        ).start()

    @pl.when(core == h)
    def _():
        c_wait(1)
        text_begin()

    mod_at = lax.broadcasted_iota(jnp.int32, (8, depth), 0)
    coef_lhs = jnp.where(mod_at == 0, 1.0 + tmod_ref[1:2, :], jnp.where(mod_at == 1, tmod_ref[0:1, :], 0.0))
    coef_lhs = jnp.concatenate(split_high_low(coef_lhs), axis=0)

    for hh in range(heads_here):
        product = dot_f32(coef_lhs, weight_of(wt_ref, hh))
        coef[hh] = product[0:2] + product[8:10]
    kbuf[s] = coef[chip]

    def coef_go(j, carry):
        @pl.when(j != s)
        def _():
            remote(coef.at[lax.div(j, 2)], kbuf.at[s], k_send, k_recv, (j, h)).start()

        return carry

    lax.fori_loop(0, seq_n, coef_go, 0)

    @pl.when(core != h)
    def _():
        c_wait(0)
        c_wait(1)
        text_begin()

    @pl.when(s < seq_n - 1)
    def _():
        for copy in up:
            copy.wait_recv()

    @pl.when(s > 0)
    def _():
        for copy in down:
            copy.wait_recv()

    side.wait_recv()
    blocks = []
    lane = lanes_of((8, 128))
    conv_bias = jnp.concatenate([convb_ref[...], jnp.zeros((1, 112), jnp.float32)], axis=1)
    for row in range(2):
        rims = zlow if row == 0 else zhigh
        mine = zown[1 + row] + rims[0]
        other = zside[row] + rims[1]
        cols = [mine[8 * i : 8 * i + 8] for i in range(line // 8)]
        left = jnp.where(h == 1, other[line - 8 : line], 0.0)
        right = jnp.where(h == 0, other[0:8], 0.0)
        cols = [left] + cols + [right]
        for i in range(line // 8):
            got = cols[i] + pltpu.roll(cols[i + 1], 128 - 16, 1) + pltpu.roll(cols[i + 2], 128 - 32, 1)
            got = jnp.where(lane < 16, got + conv_bias, 0.0)
            at = 16 * (2 * row + i % 2)
            blocks.append(got if at == 0 else pltpu.roll(got, at, 1))
    per_row = line // 8
    tokens = [
        blocks[2 * q] + blocks[2 * q + 1] + blocks[per_row + 2 * q] + blocks[per_row + 2 * q + 1]
        for q in range(per_row // 2)
    ]
    patches = jnp.concatenate(tokens, axis=0).astype(jnp.bfloat16)
    hidden = dot_f32(patches[:, : pw_ref.shape[0]], pw_ref[...]) + pb_ref[...]
    center = jnp.mean(hidden, axis=1, keepdims=True)
    offset = hidden - center
    spread_of = jnp.mean(offset * offset, axis=1, keepdims=True)
    rstd = lax.rsqrt(spread_of + eps_norm)
    hidden_ref[...] = hidden
    r_high = rstd.astype(jnp.bfloat16).astype(jnp.float32)
    r_mid = (rstd - r_high).astype(jnp.bfloat16).astype(jnp.float32)
    r_low = rstd - r_high - r_mid
    lane = lanes_of((own_rows, 128))
    block = patches.astype(jnp.float32)
    for at, value in ((64, jnp.ones_like(rstd)), (65, r_high), (66, r_mid), (67, r_low)):
        block = jnp.where(lane == at, value, block)
    psrc[...] = block.astype(jnp.bfloat16)
    pbuf[my_same] = psrc[...]
    p_begin()

    wout_copy.start()

    def tz_copy(dz):
        peer = lax.rem(z + dz, z_n)
        return remote(
            tzsend.at[peer],
            tzbuf.at[dz],
            tz_send,
            tz_recv,
            (peer * NEAR + lax.rem(s, NEAR), h),
        )

    def text_sum(i):
        peer = peer_of(i)
        mine = text_piece(x, peer)
        tx_copy(i).wait_recv()
        return mine + txbuf[peer].astype(jnp.float32)

    def text_on(i):
        tzsend[peer_of(i)] = text_sum(i).astype(jnp.bfloat16)
        tz_copy(ways[i]).start()

    text_on(0)
    text_on(1)

    for i in range(2, z_n - 1):
        text_on(i)

    wait_bytes(fzbuf.at[pl.ds(1, z_n - 1)], fz_recv)
    fold_half = fold_sum(z)
    for dz in range(1, z_n):
        fold_half = fold_half + fzbuf[dz].astype(jnp.float32)
    ffull[half_rows(core), :] = fold_half
    fold_copy = remote(
        ffull.at[half_rows(core), :], ffull.at[half_rows(core), :], m_send.at[4], m_recv.at[4], sibling
    )
    fold_copy.start()
    remote(
        ffull.at[half_rows(core), :], ffull.at[half_rows(1 - core), :], m_send.at[4], m_recv.at[4], sibling
    ).wait_recv()
    fold = ffull[...]
    shift = fold[68:69, :]
    row_at = lax.broadcasted_iota(jnp.int32, fold.shape, 0)
    fold_high, fold_low = split_high_low(jnp.where(row_at < 65, fold, 0.0))
    p_arrive()
    all_tokens = pbuf[...].reshape(same_n * own_rows, 128)
    tail = all_tokens[:, 64:].astype(jnp.float32)
    scale_of = tail[:, 1:2] + tail[:, 2:3] + tail[:, 3:4]
    tokens_in = all_tokens[:, : fold.shape[0]]
    qkv = (dot_f32(tokens_in, fold_high) + dot_f32(tokens_in, fold_low)) * scale_of + shift
    qkv = qkv.astype(jnp.bfloat16)
    query = qkv[:, :HD]
    ikv[core] = qkv[:, HD:]
    image_copy = remote(ikv.at[core], ikv.at[core], m_send.at[6], m_recv.at[6], sibling)
    image_copy.start()
    pair = head_n * own_rows

    text_own = text_sum(z_n - 1)
    stat_wait(s_recv)
    wait_bytes(kbuf.at[pl.ds(0, seq_n - 1)], k_recv)
    text_sums = jnp.sum(sbuf[...], axis=0)
    sum_at = lax.broadcasted_iota(jnp.int32, (8, half), 0)
    text_sums = jnp.where(sum_at == 0, text_sums[0:1], text_sums[1:2])
    text_sums = jnp.transpose(text_sums) / width_full
    text_mean = text_sums[:, 0:1]
    text_scale = lax.rsqrt(text_sums[:, 1:2] - text_mean * text_mean + eps_norm)
    means_apart = sbuf[...][:, 0, :] / depth - jnp.sum(sbuf[...], axis=0)[0:1] / width_full
    coefs = kbuf[...]
    centred_off = jnp.dot(
        jnp.transpose(means_apart),
        coefs[:, 0, :],
        preferred_element_type=jnp.float32,
        precision=lax.Precision.HIGHEST,
    )
    text_shift = jnp.sum(coefs, axis=0)[1:2]

    def attend(scores, values_of):
        top = jnp.max(scores, axis=1, keepdims=True)
        probs = jnp.exp(scores - top)
        return top, jnp.sum(probs, axis=1, keepdims=True), dot_f32(probs.astype(jnp.bfloat16), values_of)

    remote(ikv.at[core], ikv.at[1 - core], m_send.at[6], m_recv.at[6], sibling).wait_recv()
    image_kv = ikv[...].reshape(-1, 2 * HD)
    image_scores = dot_minor(query, image_kv[:, :HD]) / HD
    image_top, image_total, image_part = attend(image_scores, image_kv[:, HD:])

    wait_bytes(tzbuf.at[pl.ds(1, z_n - 1)], tz_recv)
    for dz in range(1, z_n):
        text_own = text_own + tzbuf[dz].astype(jnp.float32)
    text_own = (text_own + centred_off) * text_scale + text_shift
    tkv[core] = text_own.astype(jnp.bfloat16)
    text_copy = remote(tkv.at[core], tkv.at[core], m_send.at[5], m_recv.at[5], sibling)
    text_copy.start()
    remote(tkv.at[core], tkv.at[1 - core], m_send.at[5], m_recv.at[5], sibling).wait_recv()
    text_kv = tkv[...].reshape(-1, 2 * HD)
    text_scores = dot_minor(query, text_kv[:, :HD]) / HD
    text_scores = jnp.where(lanes_of(text_scores.shape) < len_ref[0], text_scores, -1e30)
    text_top, text_total, text_part = attend(text_scores, text_kv[:, HD:])
    top = jnp.maximum(image_top, text_top)
    image_share, text_share = jnp.exp(image_top - top), jnp.exp(text_top - top)
    totals = image_total * image_share + text_total * text_share
    attended = (image_part * image_share + text_part * text_share) / totals
    attended = attended.astype(jnp.bfloat16)
    attsend[...] = attended.reshape(heads_here, pair, HD)

    def a_copy(k, owner):
        return remote(
            attsend.at[k],
            attrecv.at[:, pl.ds(pl.multiple_of(owner * HD, HD), HD)],
            a_send,
            a_recv,
            (2 * k + core, h),
        )

    for off in range(1, heads_here):
        a_copy(lax.rem(chip + off, heads_here), chip).start()
    attrecv[:, pl.ds(pl.multiple_of(chip * HD, HD), HD)] = attsend[chip]
    wout_copy.wait()
    wait_bytes(attsend.at[pl.ds(0, heads_here - 1)], a_recv)

    rows = attrecv[...]
    chunks = y_send.shape[0]
    chunk = width_full // chunks

    def y_copy(j):
        at = pl.ds(j * chunk, chunk)
        return remote(
            ysend.at[:, at], yrecv.at[:, at], y_send.at[j], y_recv.at[j], (s, 1 - h)
        )

    for j in range(chunks):
        part = dot_f32(rows, woutv[:, j * chunk : (j + 1) * chunk])
        first, second = part[:own_rows], part[own_rows:]
        ysend[:, j * chunk : (j + 1) * chunk] = jnp.where(h == 0, second, first).astype(jnp.bfloat16)
        proj[:, j * chunk : (j + 1) * chunk] = jnp.where(h == 0, first, second)
        y_copy(j).start()
    def out_copy(j):
        at = pl.ds(j * chunk, chunk)
        return pltpu.make_async_copy(out_ref.at[:, at], out_hbm.at[:, at], out_sem.at[j])

    g_sent()
    p_sent()

    stat_wait(s_send)
    wait_bytes(kbuf.at[pl.ds(0, seq_n - 1)], k_send)
    far_copy.wait_send()

    @pl.when(core != h)
    def _():
        near_copy.wait_send()

    for copy in (w_copy, mod_copy, pair_copy, fx_copy, fold_copy, image_copy, text_copy, side):
        copy.wait_send()

    @pl.when(s > 0)
    def _():
        for copy in up:
            copy.wait_send()

    @pl.when(s < seq_n - 1)
    def _():
        for copy in down:
            copy.wait_send()

    wait_bytes(fzbuf.at[pl.ds(0, z_n - 1)], fz_send)
    wait_bytes(tzbuf.at[pl.ds(0, z_n - 1)], tz_send)
    wait_bytes(tstage, tx_send)
    wait_bytes(attsend.at[pl.ds(0, heads_here - 1)], a_send)
    for j in range(chunks):
        y_copy(j).wait_recv()
        at = slice(j * chunk, (j + 1) * chunk)
        projected = proj[:, at] + yrecv[:, at].astype(jnp.float32) + ob_ref[:, at]
        out_ref[:, at] = (hidden_ref[:, at] + mod_ref[2:3, at] * projected).astype(jnp.bfloat16)
        out_copy(j).start()
    for j in range(chunks):
        y_copy(j).wait_send()
        out_copy(j).wait()


def fused_body(
    features,
    gn_gain,
    gn_bias,
    conv_weight,
    conv_bias,
    patch_weight,
    patch_bias,
    image_mod,
    w_qkv,
    text_ids,
    text_length,
    text_table,
    text_mod,
    w_text,
    w_out,
    out_bias,
):
    frame_count, row_count, col_count, chan_count = features.shape
    width_full = patch_weight.shape[1]
    seq_n, head_n = lax.axis_size("seq"), lax.axis_size("head")
    depth, _, head_width = w_qkv.shape
    heads_here = head_width // HD
    z_n = seq_n // NEAR
    cells = frame_count * row_count * col_count
    own = cells // 4
    half = text_ids.shape[0] // 2
    count = seq_n * head_n
    f32, bf16 = jnp.float32, jnp.bfloat16

    anywhere = pl.BlockSpec(memory_space=pl.ANY)
    sems = pltpu.SemaphoreType.DMA
    scratch = pltpu.VMEM
    line = cells // 2
    fold_shape = (48, 3 * HD)
    out = pl.pallas_call(
        functools.partial(fused_kernel, seq_n, head_n, cells * (chan_count // GN_GROUPS) * count),
        out_shape=jax.ShapeDtypeStruct((own, width_full), bf16),
        in_specs=[anywhere, pl.BlockSpec(memory_space=pltpu.SMEM)] + [anywhere] * 14,
        out_specs=anywhere,
        scratch_shapes=[
            scratch((depth, 2 * head_width), bf16),
            scratch((own, width_full), bf16),
            scratch(features.shape, bf16),
            scratch(patch_weight.shape, bf16),
            scratch((1, width_full), f32),
            scratch(image_mod.shape, f32),
            scratch((1, text_ids.shape[0]), jnp.int32),
            scratch((1, chan_count), f32),
            scratch((1, chan_count), f32),
            scratch((27 * conv_bias.shape[0], chan_count), bf16),
            scratch((1, conv_bias.shape[0]), f32),
            scratch(text_mod.shape, f32),
            scratch((1, width_full), f32),
            scratch((cells, chan_count), f32),
            scratch((depth, text_table.shape[1]), bf16),
            scratch((3, depth, head_width), bf16),
            scratch((depth, half), bf16),
            scratch((2, half), f32),
            scratch((8, 128), f32),
            scratch((count, 8, 128), f32),
            scratch((4, line, 128), f32),
            scratch((2, line, 128), f32),
            scratch((2, line, 128), f32),
            scratch((2, line, 128), f32),
            scratch((own, 128), bf16),
            scratch((count // 2, own, 128), bf16),
            scratch((seq_n, 2, half), f32),
            scratch((heads_here, 2, 2 * HD), f32),
            scratch((seq_n, 2, 2 * HD), f32),
            scratch((2, depth, half), bf16),
            scratch((depth, 2 * head_width), bf16),
            scratch((2, depth), f32),
            scratch((4, half, depth), bf16),
            scratch((heads_here, 2 * fold_shape[0], 3 * HD), f32),
            scratch((heads_here, *fold_shape), f32),
            scratch((z_n, *fold_shape), bf16),
            scratch((z_n, *fold_shape), bf16),
            scratch((z_n, *fold_shape), bf16),
            scratch((z_n, *fold_shape), bf16),
            scratch((2 * fold_shape[0], 3 * HD), f32),
            scratch((z_n, half, 2 * HD), bf16),
            scratch((z_n, half, 2 * HD), bf16),
            scratch((z_n, half, 2 * HD), bf16),
            scratch((z_n, half, 2 * HD), bf16),
            scratch((2, half, 2 * HD), bf16),
            scratch((2, count * own // 2, 2 * HD), bf16),
            scratch((heads_here, head_n * own, HD), bf16),
            scratch((head_n * own, head_width), bf16),
            scratch((own, width_full), f32),
            scratch((own, width_full), bf16),
            scratch((own, width_full), bf16),
            scratch((own, width_full), f32),
            scratch((head_width, width_full), bf16),
            sems((12,)),
            sems((4,)),
            sems((8,)),
            sems,
            sems,
            sems,
            sems,
            sems,
            sems,
            sems,
            sems,
            sems,
            sems,
            sems((2,)),
            sems((2,)),
            sems((7,)),
            sems((7,)),
            sems((5,)),
            sems((5,)),
            sems,
            sems,
            sems,
            sems((z_n,)),
            sems,
            sems,
            sems,
            sems,
            sems((4,)),
            sems((4,)),
        ],
        compiler_params=pltpu.CompilerParams(
            collective_id=3, has_side_effects=True, vmem_limit_bytes=60 * 1024 * 1024
        ),
    )(
        w_text.reshape(depth, 2 * head_width),
        text_length,
        features,
        patch_weight,
        patch_bias[None],
        image_mod,
        text_ids[None],
        gn_gain[None],
        gn_bias[None],
        conv_weight.reshape(-1, chan_count),
        conv_bias[None],
        text_mod,
        out_bias[None],
        text_table,
        w_qkv.transpose(1, 0, 2),
        w_out,
    )
    out = out.reshape(col_count // 2, frame_count, width_full).transpose(1, 0, 2)
    return out.reshape(frame_count, row_count // 2, col_count // 2, width_full)


def choose_body(*operands):
    features, w_qkv = operands[0], operands[8]
    seq_n, head_n = lax.axis_size("seq"), lax.axis_size("head")
    pair = seq_n == 2 * (w_qkv.shape[2] // HD) and head_n == 2 and seq_n % NEAR == 0
    small = features.shape[:3] == (8, 2, 4) and features.shape[3] == 512
    return fused_body(*operands) if pair and small else body(*operands)


def solution(mesh):
    return jax.shard_map(
        choose_body,
        mesh=mesh,
        in_specs=(
            P(None, "seq", "head", None),
            P(),
            P(),
            P(),
            P(),
            P(),
            P(),
            P(),
            P("seq", None, "head"),
            P(),
            P(),
            P("seq", None),
            P(None, "seq"),
            P("seq", None, "head"),
            P("head", None),
            P(),
        ),
        out_specs=P(None, "seq", "head", None),
        check_vma=False,
    )
```

```python
import functools

import jax
import jax.numpy as jnp
from jax import lax
from jax.experimental import pallas as pl
from jax.experimental.pallas import tpu as pltpu
from jax.sharding import PartitionSpec as P

HD = 128
GN_GROUPS = 32
CHUNK = 512

eps_norm = 1e-06


MESH = pl.DeviceIdType.MESH


def place_of(index, head_n):
    return (lax.div(index, head_n), lax.rem(index, head_n))


def greet_all(seq_n, head_n):
    count = seq_n * head_n
    me = lax.axis_index("seq") * head_n + lax.axis_index("head")
    barrier = pltpu.get_barrier_semaphore()

    def greet(off, carry):
        pl.semaphore_signal(
            barrier,
            inc=1,
            device_id=place_of(lax.rem(me + off, count), head_n),
            device_id_type=MESH,
        )
        return carry

    lax.fori_loop(1, count, greet, 0)
    pl.semaphore_wait(barrier, count - 1)


def start_share(seq_n, head_n, x_ref, out_ref, local_sem, send_sem, recv_sem):
    count = seq_n * head_n
    me = lax.axis_index("seq") * head_n + lax.axis_index("head")

    def copy(off, slot):
        return pltpu.make_async_remote_copy(
            src_ref=x_ref,
            dst_ref=out_ref.at[slot],
            send_sem=send_sem.at[off],
            recv_sem=recv_sem.at[off],
            device_id=place_of(lax.rem(me + off, count), head_n),
            device_id_type=MESH,
        )

    def send(off, carry):
        copy(off, me).start()
        return carry

    lax.fori_loop(1, count, send, 0)
    own = pltpu.make_async_copy(x_ref, out_ref.at[me], local_sem)
    own.start()

    def finish():
        own.wait()

        def wait(off, carry):
            copy(off, me).wait_send()
            copy(off, lax.rem(me + count - off, count)).wait_recv()
            return carry

        lax.fori_loop(1, count, wait, 0)

    return finish


def share_kernel(seq_n, head_n, x_ref, out_ref, local_sem, send_sem, recv_sem):
    greet_all(seq_n, head_n)
    start_share(seq_n, head_n, x_ref, out_ref, local_sem, send_sem, recv_sem)()


def swap_kernel(seq_n, x_ref, out_ref, local_sem, send_sem, recv_sem):
    me, h = lax.axis_index("seq"), lax.axis_index("head")
    barrier = pltpu.get_barrier_semaphore()

    def greet(off, carry):
        pl.semaphore_signal(
            barrier, inc=1, device_id=(lax.rem(me + off, seq_n), h), device_id_type=MESH
        )
        return carry

    lax.fori_loop(1, seq_n, greet, 0)
    pl.semaphore_wait(barrier, seq_n - 1)

    def copy(off, slot):
        peer = lax.rem(me + off, seq_n)
        return pltpu.make_async_remote_copy(
            src_ref=x_ref.at[peer],
            dst_ref=out_ref.at[slot],
            send_sem=send_sem.at[off],
            recv_sem=recv_sem.at[off],
            device_id=(peer, h),
            device_id_type=MESH,
        )

    def send(off, carry):
        copy(off, me).start()
        return carry

    lax.fori_loop(1, seq_n, send, 0)
    own = pltpu.make_async_copy(x_ref.at[me], out_ref.at[me], local_sem)
    own.start()
    own.wait()

    def wait(off, carry):
        copy(off, me).wait_send()
        copy(off, lax.rem(me + seq_n - off, seq_n)).wait_recv()
        return carry

    lax.fori_loop(1, seq_n, wait, 0)


def swap(x):
    seq_n = lax.axis_size("seq")
    return pl.pallas_call(
        functools.partial(swap_kernel, seq_n),
        out_shape=jax.ShapeDtypeStruct(x.shape, x.dtype),
        in_specs=[pl.BlockSpec(memory_space=pltpu.VMEM)],
        out_specs=pl.BlockSpec(memory_space=pltpu.VMEM),
        scratch_shapes=[
            pltpu.SemaphoreType.DMA,
            pltpu.SemaphoreType.DMA((seq_n,)),
            pltpu.SemaphoreType.DMA((seq_n,)),
        ],
        compiler_params=pltpu.CompilerParams(collective_id=1, has_side_effects=True),
    )(x)


def share(x, collective_id):
    seq_n, head_n = lax.axis_size("seq"), lax.axis_size("head")
    count = seq_n * head_n
    return pl.pallas_call(
        functools.partial(share_kernel, seq_n, head_n),
        out_shape=jax.ShapeDtypeStruct((count, *x.shape), x.dtype),
        in_specs=[pl.BlockSpec(memory_space=pltpu.VMEM)],
        out_specs=pl.BlockSpec(memory_space=pltpu.VMEM),
        scratch_shapes=[
            pltpu.SemaphoreType.DMA,
            pltpu.SemaphoreType.DMA((count,)),
            pltpu.SemaphoreType.DMA((count,)),
        ],
        compiler_params=pltpu.CompilerParams(collective_id=collective_id, has_side_effects=True),
    )(x)


def weights_kernel(
    heads_here,
    group,
    wq_ref,
    wt_ref,
    ctx_ref,
    x_ref,
    w_ref,
    full_ref,
    parts_ref,
    local_sem,
    send_sem,
    recv_sem,
    pass_send,
    pass_recv,
    share_local,
    share_send,
    share_recv,
):
    s, h = lax.axis_index("seq"), lax.axis_index("head")
    mine, place = lax.div(s, group), lax.rem(s, group)
    width = heads_here * HD
    greet_all(lax.axis_size("seq"), lax.axis_size("head"))
    finish_share = start_share(
        lax.axis_size("seq"), lax.axis_size("head"), x_ref, parts_ref, share_local, share_send, share_recv
    )

    def pieces(head, slot):
        out = []
        for i in range(5):
            ref, at = (wq_ref, i) if i < 3 else (wt_ref, i - 3)
            start = pl.multiple_of(at * width + head * HD, HD)
            out.append((ref.at[:, pl.ds(start, HD)], w_ref.at[slot, :, pl.ds(i * HD, HD)]))
        out.append((ctx_ref, full_ref.at[slot]))
        return out

    def first(off, slot):
        head = lax.rem(mine + off, heads_here)
        return [
            pltpu.make_async_remote_copy(
                src_ref=src,
                dst_ref=dst,
                send_sem=send_sem.at[off, i],
                recv_sem=recv_sem.at[off, i],
                device_id=(head * group + place, h),
                device_id_type=MESH,
            )
            for i, (src, dst) in enumerate(pieces(head, slot))
        ]

    def second(off, piece, slot):
        peer = mine * group + lax.rem(place + off, group)
        return [
            pltpu.make_async_remote_copy(
                src_ref=ref.at[slot],
                dst_ref=ref.at[slot],
                send_sem=pass_send.at[off, piece, i],
                recv_sem=pass_recv.at[off, piece, i],
                device_id=(peer, h),
                device_id_type=MESH,
            )
            for i, ref in enumerate((w_ref, full_ref))
        ]

    for off in range(1, heads_here):
        for copy in first(off, s):
            copy.start()
    own = [
        pltpu.make_async_copy(src, dst, local_sem.at[i])
        for i, (src, dst) in enumerate(pieces(mine, s))
    ]
    for copy in own:
        copy.start()
    for copy in own:
        copy.wait()
    for piece in range(heads_here):
        slot = lax.rem(mine + heads_here - piece, heads_here) * group + place
        if piece > 0:
            for copy in first(piece, slot):
                copy.wait_recv()
        for off in range(1, group):
            for copy in second(off, piece, slot):
                copy.start()
    for off in range(1, heads_here):
        for copy in first(off, s):
            copy.wait_send()
    for piece in range(heads_here):
        from_group = lax.rem(mine + heads_here - piece, heads_here) * group
        for off in range(1, group):
            for copy in second(off, piece, from_group + place):
                copy.wait_send()
            for copy in second(off, piece, from_group + lax.rem(place + group - off, group)):
                copy.wait_recv()
    finish_share()


def gather_weights(w_qkv, w_text, own_context, shares):
    seq_n = lax.axis_size("seq")
    depth, _, head_width = w_qkv.shape
    heads_here = head_width // HD
    group = seq_n // heads_here
    count = seq_n * lax.axis_size("head")
    text_count = own_context.shape[1]
    anywhere = pl.BlockSpec(memory_space=pl.ANY)
    sems = pltpu.SemaphoreType.DMA
    return pl.pallas_call(
        functools.partial(weights_kernel, heads_here, group),
        out_shape=(
            jax.ShapeDtypeStruct((seq_n, depth, 5 * HD), w_qkv.dtype),
            jax.ShapeDtypeStruct((seq_n, depth, text_count), own_context.dtype),
            jax.ShapeDtypeStruct((count, *shares.shape), shares.dtype),
        ),
        in_specs=[anywhere] * 3 + [pl.BlockSpec(memory_space=pltpu.VMEM)],
        out_specs=(anywhere, anywhere, pl.BlockSpec(memory_space=pltpu.VMEM)),
        scratch_shapes=[
            sems((6,)),
            sems((heads_here, 6)),
            sems((heads_here, 6)),
            sems((group, heads_here, 2)),
            sems((group, heads_here, 2)),
            sems,
            sems((count,)),
            sems((count,)),
        ],
        compiler_params=pltpu.CompilerParams(collective_id=2, has_side_effects=True),
    )(w_qkv.reshape(depth, 3 * head_width), w_text.reshape(depth, 2 * head_width), own_context, shares)


def group_norm(features, gn_gain, gn_bias, text_mod):
    frame_count, row_count, col_count, chan_count = features.shape
    per_group = chan_count // GN_GROUPS
    values = features.astype(jnp.float32)
    chan_sums = jnp.stack(
        [jnp.sum(values, axis=(0, 1, 2)), jnp.sum(values * values, axis=(0, 1, 2))]
    )
    sums = jnp.sum(chan_sums.reshape(2, GN_GROUPS, per_group), axis=2)
    seq_n, head_n = lax.axis_size("seq"), lax.axis_size("head")
    depth = text_mod.shape[1]
    lines = -(-depth // 128)
    mod = jnp.pad(text_mod, ((0, 0), (0, lines * 128 - depth))).reshape(2 * lines, 128)
    block = jnp.concatenate([jnp.pad(sums, ((0, 0), (0, 128 - GN_GROUPS))), mod], axis=0)
    block = jnp.pad(block, ((0, -block.shape[0] % 8), (0, 0)))
    shared = share(block, 0)
    sums = jnp.sum(shared[:, :2, :GN_GROUPS], axis=0)
    mod = shared.reshape(seq_n, head_n, -1, 128)[:, 0, 2 : 2 + 2 * lines]
    mod = mod.reshape(seq_n, 2, lines * 128)[:, :, :depth]
    mod = mod.transpose(1, 0, 2).reshape(2, seq_n * depth)
    cell_count = (
        frame_count * row_count * col_count * per_group * lax.axis_size("seq") * lax.axis_size("head")
    )
    mean = sums[0] / cell_count
    scale = lax.rsqrt(sums[1] / cell_count - mean * mean + eps_norm)
    mean = jnp.repeat(mean, per_group)
    scale = jnp.repeat(scale, per_group)
    normed = (values - mean) * scale
    return jax.nn.silu(normed * gn_gain + gn_bias).astype(jnp.bfloat16), mod


def join_rims(parts, block_dim, dim, unit):
    size = parts.shape[dim]
    blocks = parts.shape[block_dim]
    core = lax.slice_in_dim(parts, unit, size - unit, axis=dim)
    low = lax.slice_in_dim(parts, 0, unit, axis=dim)
    high = lax.slice_in_dim(parts, size - unit, size, axis=dim)
    low = lax.slice_in_dim(low, 1, blocks, axis=block_dim)
    high = lax.slice_in_dim(high, 0, blocks - 1, axis=block_dim)
    pad_low = [(0, 0)] * parts.ndim
    pad_low[block_dim] = (0, 1)
    pad_low[dim] = (size - 3 * unit, 0)
    pad_high = [(0, 0)] * parts.ndim
    pad_high[block_dim] = (1, 0)
    pad_high[dim] = (0, size - 3 * unit)
    return core + jnp.pad(low, pad_low) + jnp.pad(high, pad_high)


def conv_shares(activated, conv_weight):
    padded = jnp.concatenate([activated[:1], activated[:1], activated], axis=0)
    shares = lax.conv_general_dilated(
        padded[None],
        conv_weight,
        (1, 1, 1),
        ((0, 0), (2, 2), (2, 2)),
        dimension_numbers=("NDHWC", "DHWOI", "NDHWC"),
        preferred_element_type=jnp.float32,
    )[0]
    return shares.reshape(-1, 128)


def all_patches(parts, frame_count, row_count, col_count, conv_bias):
    seq_n, head_n = lax.axis_size("seq"), lax.axis_size("head")
    chans = conv_bias.shape[0]
    parts = parts.reshape(
        seq_n, head_n, frame_count, row_count + 2, (col_count + 2) * chans
    )
    parts = join_rims(join_rims(parts, 0, 3, 1), 1, 4, chans)
    latent = (parts + jnp.tile(conv_bias, col_count)).astype(jnp.bfloat16)
    blocks = latent.reshape(
        seq_n, head_n, frame_count, row_count // 2, 2, col_count // 2, 2 * chans
    )
    blocks = blocks.transpose(0, 1, 2, 3, 5, 4, 6)
    own = frame_count * (row_count // 2) * (col_count // 2)
    return blocks.reshape(seq_n * head_n * own, 4 * chans)


def modulate(patches, patch_weight, patch_bias, image_mod):
    hidden = jnp.dot(patches, patch_weight, preferred_element_type=jnp.float32) + patch_bias
    center = jnp.mean(hidden, axis=1, keepdims=True)
    offset = hidden - center
    spread = jnp.mean(offset * offset, axis=1, keepdims=True)
    normed = offset * lax.rsqrt(spread + eps_norm)
    return (normed * (1.0 + image_mod[1]) + image_mod[0]).astype(jnp.bfloat16)


def body(
    features,
    gn_gain,
    gn_bias,
    conv_weight,
    conv_bias,
    patch_weight,
    patch_bias,
    image_mod,
    w_qkv,
    text_ids,
    text_length,
    text_table,
    text_mod,
    w_text,
    w_out,
    out_bias,
):
    frame_count, row_count, col_count, _ = features.shape
    width_full = patch_weight.shape[1]
    seq_n, head_n = lax.axis_size("seq"), lax.axis_size("head")
    seq_i, head_i = lax.axis_index("seq"), lax.axis_index("head")
    depth, _, head_width = w_qkv.shape
    heads_here = head_width // HD
    group = seq_n // heads_here
    text_count = text_ids.shape[0]

    chosen = (
        lax.broadcasted_iota(jnp.int32, (text_table.shape[1], text_count), 0) == text_ids[None, :]
    ).astype(jnp.bfloat16)
    own_context = jnp.dot(text_table, chosen, preferred_element_type=jnp.float32).astype(
        jnp.bfloat16
    )
    activated, mod = group_norm(features, gn_gain, gn_bias, text_mod)
    shares = conv_shares(activated, conv_weight)
    weights, context, parts = gather_weights(w_qkv, w_text, own_context, shares)
    weights = weights.reshape(width_full, 5 * HD)
    context = context.reshape(width_full, text_count).astype(jnp.float32)
    text_mean = jnp.sum(context, axis=0) / width_full
    text_square = jnp.sum(context * context, axis=0) / width_full
    text_scale = lax.rsqrt(text_square - text_mean * text_mean + eps_norm)
    text_normed = (context - text_mean) * text_scale * (1.0 + mod[1][:, None]) + mod[0][:, None]
    text_high = text_normed.astype(jnp.bfloat16)
    text_low = (text_normed - text_high.astype(jnp.float32)).astype(jnp.bfloat16)
    w_text_flat = weights[:, 3 * HD :]
    text_kv = sum(
        lax.dot_general(
            part, w_text_flat, (((0,), (0,)), ((), ())), preferred_element_type=jnp.float32
        )
        for part in (text_high, text_low)
    ).astype(jnp.bfloat16)

    patches = all_patches(parts, frame_count, row_count, col_count, conv_bias)
    own = patches.shape[0] // (seq_n * head_n)
    part_rows = head_n * own // group
    my_part = seq_i % group
    chunk = min(CHUNK, patches.shape[0])

    def project(rows):
        modulated = modulate(rows, patch_weight, patch_bias, image_mod)
        qkv = jnp.dot(modulated, weights[:, : 3 * HD], preferred_element_type=jnp.float32)
        query, kv = qkv[:, :HD], qkv[:, HD:]
        query = lax.dynamic_index_in_dim(
            query.reshape(-1, group, part_rows, HD), my_part, axis=1, keepdims=False
        )
        return kv.astype(jnp.bfloat16), query.reshape(-1, HD).astype(jnp.bfloat16)

    if chunk == patches.shape[0]:
        image_kv, query = project(patches)
    else:
        image_kv, query = lax.map(project, patches.reshape(-1, chunk, patches.shape[1]))
        image_kv = image_kv.reshape(-1, 2 * HD)
        query = query.reshape(-1, HD)

    keys = jnp.concatenate([image_kv[:, :HD], text_kv[:, :HD]], axis=0)
    vals = jnp.concatenate([image_kv[:, HD:], text_kv[:, HD:]], axis=0)
    key_valid = (
        jnp.arange(keys.shape[0], dtype=jnp.int32) < image_kv.shape[0] + text_length[0]
    )
    scores = (
        lax.dot_general(query, keys, (((1,), (1,)), ((), ())), preferred_element_type=jnp.float32)
        / HD
    )
    scores = jnp.where(key_valid[None, :], scores, -1e30)
    probs = jnp.exp(scores - jnp.max(scores, axis=1, keepdims=True))
    totals = jnp.sum(probs, axis=1, keepdims=True)
    attended = (
        jnp.dot(probs.astype(jnp.bfloat16), vals, preferred_element_type=jnp.float32) / totals
    ).astype(jnp.bfloat16)

    attended = attended.reshape(seq_n, part_rows, HD)
    attended = swap(attended)
    attended = attended.reshape(heads_here, group, part_rows, HD).transpose(1, 2, 0, 3)
    attended = attended.reshape(head_n * own, head_width)
    if head_n == 2:
        halves = jnp.dot(attended, w_out, preferred_element_type=jnp.float32)
        halves = halves.reshape(2, own, width_full)
        away = lax.dynamic_index_in_dim(halves, 1 - head_i, 0, keepdims=False)
        here = lax.dynamic_index_in_dim(halves, head_i, 0, keepdims=False)
        projected = here + lax.ppermute(away, "head", [(0, 1), (1, 0)]) + out_bias
    else:
        projected = (
            lax.psum_scatter(
                jnp.dot(attended, w_out, preferred_element_type=jnp.float32),
                "head",
                scatter_dimension=0,
                tiled=True,
            )
            + out_bias
        )
    own_patches = lax.dynamic_slice_in_dim(patches, (seq_i * head_n + head_i) * own, own, axis=0)
    hidden = jnp.dot(own_patches, patch_weight, preferred_element_type=jnp.float32) + patch_bias
    block_out = (hidden + image_mod[2] * projected).astype(jnp.bfloat16)
    return block_out.reshape(frame_count, row_count // 2, col_count // 2, width_full)


NEAR = 4


def lanes_of(shape):
    return lax.broadcasted_iota(jnp.int32, shape, len(shape) - 1)


def group_sum(values, per_group):
    lane = lanes_of(values.shape)
    width = values.shape[-1]
    step = 1
    while step < per_group:
        above = pltpu.roll(values, width - step, 1)
        below = pltpu.roll(values, step, 1)
        values = values + jnp.where(lax.rem(lax.div(lane, step), 2) == 0, above, below)
        step *= 2
    return values


def split_high_low(values):
    high = values.astype(jnp.bfloat16)
    return high, (values - high.astype(jnp.float32)).astype(jnp.bfloat16)


def dot_f32(a, b):
    return jnp.dot(a, b, preferred_element_type=jnp.float32)


def dot_minor(a, b):
    return lax.dot_general(a, b, (((1,), (1,)), ((), ())), preferred_element_type=jnp.float32)


def fused_kernel(
    seq_n,
    head_n,
    cell_count,
    wt_hbm,
    len_ref,
    x_hbm,
    pw_hbm,
    pb_hbm,
    mod_hbm,
    ids_hbm,
    gain_hbm,
    bias_hbm,
    convw_hbm,
    convb_hbm,
    tmod_hbm,
    ob_hbm,
    table_ref,
    wq_ref,
    wout_ref,
    out_hbm,
    wt_ref,
    out_ref,
    x_raw,
    pw_ref,
    pb_ref,
    mod_ref,
    ids_ref,
    gain_ref,
    bias_ref,
    convw_ref,
    convb_ref,
    tmod_ref,
    ob_ref,
    spots,
    tablev,
    wqv,
    ctx_ref,
    stat_ref,
    gsrc,
    gbuf,
    zown,
    zlow,
    zhigh,
    zside,
    psrc,
    pbuf,
    sbuf,
    coef,
    kbuf,
    cbuf,
    wbuf,
    mbuf,
    lhs_ref,
    fstage,
    fpair,
    fxsend,
    fxbuf,
    fzsend,
    fzbuf,
    ffull,
    tstage,
    txbuf,
    tzsend,
    tzbuf,
    tkv,
    ikv,
    attsend,
    attrecv,
    proj,
    ysend,
    yrecv,
    hidden_ref,
    woutv,
    in_sem,
    out_sem,
    table_sem,
    wq_sem,
    wout_sem,
    g_send,
    g_recv,
    p_send,
    p_recv,
    s_send,
    s_recv,
    k_send,
    k_recv,
    c_send,
    c_recv,
    m_send,
    m_recv,
    h_send,
    h_recv,
    fz_send,
    fz_recv,
    tx_send,
    tx_recv,
    tz_send,
    tz_recv,
    a_send,
    a_recv,
    y_send,
    y_recv,
):
    count = seq_n * head_n
    s, h = lax.axis_index("seq"), lax.axis_index("head")
    me = s * head_n + h
    core = lax.rem(s, 2)
    x = lax.rem(lax.div(s, 2), 2)
    z = lax.div(s, NEAR)
    z_n = seq_n // NEAR
    chip = lax.div(s, 2)
    heads_here = seq_n // 2
    sibling = (s + 1 - 2 * core, h)
    across = (s + 2 - 4 * x, h)
    depth = wt_ref.shape[0]
    width = heads_here * HD
    width_full = pw_ref.shape[1]
    own_rows = psrc.shape[0]

    def remote(src, dst, send, recv, device):
        return pltpu.make_async_remote_copy(
            src_ref=src, dst_ref=dst, send_sem=send, recv_sem=recv, device_id=device, device_id_type=MESH
        )

    pieces = table_sem.shape[0]
    piece = table_ref.shape[1] // pieces

    def table_copy(i):
        at = pl.ds(i * piece, piece)
        return pltpu.make_async_copy(table_ref.at[:, at], tablev.at[:, at], table_sem.at[i])

    wq_copy = pltpu.make_async_copy(wq_ref, wqv, wq_sem)
    wout_copy = pltpu.make_async_copy(wout_ref, woutv, wout_sem)
    small = [
        pltpu.make_async_copy(src, dst, in_sem.at[i])
        for i, (src, dst) in enumerate(
            (
                (x_hbm, x_raw),
                (pw_hbm, pw_ref),
                (pb_hbm, pb_ref),
                (mod_hbm, mod_ref),
                (ids_hbm, ids_ref),
                (gain_hbm, gain_ref),
                (bias_hbm, bias_ref),
                (convw_hbm, convw_ref),
                (convb_hbm, convb_ref),
                (tmod_hbm, tmod_ref),
                (ob_hbm, ob_ref),
                (wt_hbm, wt_ref),
            )
        )
    ]
    barrier = pltpu.get_barrier_semaphore()

    def greet(off, carry):
        pl.semaphore_signal(
            barrier, inc=1, device_id=place_of(lax.rem(me + off, count), head_n), device_id_type=MESH
        )
        return carry

    small[0].start()
    lax.fori_loop(1, count, greet, 0)

    for copy in small[1:4]:
        copy.start()
    wq_copy.start()
    small[4].start()
    for i in range(2):
        table_copy(i).start()

    frames, row_n, col_n, _ = x_raw.shape
    cells = frames * row_n * col_n
    small[0].wait()
    for i in range(2, pieces):
        table_copy(i).start()
    for copy in small[5:]:
        copy.start()
    for f in range(frames):
        for r in range(row_n):
            at = (f * row_n + r) * col_n
            spots[at : at + col_n, :] = x_raw[f, r].astype(jnp.float32)
    to_at = lax.broadcasted_iota(jnp.int32, (cells, cells), 0)
    from_at = lax.broadcasted_iota(jnp.int32, (cells, cells), 1)
    wanted = lax.rem(to_at, frames) * (row_n * col_n) + lax.div(to_at, frames)
    values = dot_f32((from_at == wanted).astype(jnp.bfloat16), spots[...].astype(jnp.bfloat16))
    chan_count = values.shape[1]
    lines = chan_count // 128
    per_group = chan_count // GN_GROUPS
    total = jnp.sum(values, axis=0, keepdims=True)
    square = jnp.sum(values * values, axis=0, keepdims=True)
    for j in range(lines):
        gsrc[j : j + 1, :] = total[:, j * 128 : (j + 1) * 128]
        gsrc[lines + j : lines + j + 1, :] = square[:, j * 128 : (j + 1) * 128]
    gbuf[me] = gsrc[...]

    pl.semaphore_wait(barrier, count - 1)

    def wait_bytes(refs, sem):
        pltpu.make_async_copy(refs, refs, sem).wait()

    def spread(src, buf, send, recv):
        def begin():
            def one(off, carry):
                remote(
                    src, buf.at[me], send, recv, place_of(lax.rem(me + off, count), head_n)
                ).start()
                return carry

            lax.fori_loop(1, count, one, 0)

        def all_of(sem):
            wait_bytes(buf.at[pl.ds(0, count - 1)], sem)

        return begin, lambda: all_of(recv), lambda: all_of(send)

    g_begin, g_arrive, g_sent = spread(gsrc, gbuf, g_send, g_recv)
    same_n = count // 2
    my_same = chip * head_n + h

    def p_begin():
        def one(off, carry):
            to_chip, to_h = place_of(lax.rem(my_same + off, same_n), head_n)
            remote(psrc, pbuf.at[my_same], p_send, p_recv, (2 * to_chip + core, to_h)).start()
            return carry

        lax.fori_loop(1, same_n, one, 0)

    def p_arrive():
        wait_bytes(pbuf.at[pl.ds(0, same_n - 1)], p_recv)

    def p_sent():
        wait_bytes(pbuf.at[pl.ds(0, same_n - 1)], p_send)

    g_begin()

    w_copy = remote(wt_hbm, wbuf, m_send.at[0], m_recv.at[0], sibling)
    w_copy.start()

    def own_features(ref, rows):
        both = ref[rows, pl.ds(pl.multiple_of(chip * 2 * depth, 128), 2 * depth)].astype(jnp.float32)
        return jnp.where(core == 0, both[:, :depth], both[:, depth:])

    def feature_mean(ref):
        return jnp.mean(ref[...].astype(jnp.float32), axis=1, keepdims=True)

    for copy in small[1:4]:
        copy.wait()
    gain = 1.0 + own_features(mod_ref, slice(1, 2))
    lines_main = (own_features(pw_ref, slice(None)) - feature_mean(pw_ref)) * gain
    line_bias = (own_features(pb_ref, slice(None)) - feature_mean(pb_ref)) * gain
    line_at = lax.broadcasted_iota(jnp.int32, (16, depth), 0)
    lines_rest = jnp.where(
        line_at == 0, line_bias, jnp.where(line_at == 4, own_features(mod_ref, slice(0, 1)), 0.0)
    )
    lines_all = jnp.concatenate([lines_main, lines_rest, jnp.zeros((16, depth), jnp.float32)], axis=0)
    fold_lhs = jnp.concatenate(split_high_low(lines_all), axis=0)
    fold_rows = fstage.shape[1]
    wq_copy.wait()
    for i in range(3):
        product = dot_f32(fold_lhs, wqv[i])
        product = product[:fold_rows] + product[fold_rows:]
        for hh in range(heads_here):
            fstage[hh, :, i * HD : (i + 1) * HD] = product[:, hh * HD : (hh + 1) * HD]

    rows_half = fpair.shape[1]

    def half_rows(which):
        return pl.ds(pl.multiple_of(which * rows_half, 8), rows_half)

    pair_copy = remote(fstage.at[:, half_rows(1 - core), :], fpair, m_send.at[2], m_recv.at[2], sibling)
    pair_copy.start()

    half = ctx_ref.shape[1]
    small[4].wait()
    ids = ids_ref[:, pl.ds(pl.multiple_of(h * half, 128), half)]
    spot = lax.broadcasted_iota(jnp.int32, (piece, half), 0)

    def look_up(i, found):
        table_copy(i).wait()
        chosen = (spot == ids - i * piece).astype(jnp.bfloat16)
        return found + dot_f32(tablev[:, i * piece : (i + 1) * piece], chosen)

    found = jnp.zeros((depth, half), jnp.float32)
    for i in range(pieces // 2):
        found = look_up(i, found)

    pair_copy.wait_recv()

    def fold_pair(xx, zz):
        return fstage[2 * zz + xx, half_rows(core), :] + fpair[2 * zz + xx]

    for zz in range(z_n):
        fxsend[zz] = fold_pair(1 - x, zz).astype(fxsend.dtype)
    fx_copy = remote(fxsend, fxbuf, m_send.at[3], m_recv.at[3], across)
    fx_copy.start()

    for i in range(pieces // 2, pieces):
        found = look_up(i, found)
    stat_ref[0:1, :] = jnp.sum(found, axis=0, keepdims=True)
    stat_ref[1:2, :] = jnp.sum(found * found, axis=0, keepdims=True)
    ctx_ref[...] = found.astype(jnp.bfloat16)

    same = core == h
    slot = jnp.where(same, 0, 1)
    there = 2 * chip + h
    near_copy = remote(ctx_ref, cbuf.at[slot], c_send.at[0], c_recv.at[slot], (there, h))
    far_copy = remote(ctx_ref, cbuf.at[slot], c_send.at[1], c_recv.at[slot], (there, 1 - h))
    far_copy.start()

    @pl.when(core != h)
    def _():
        near_copy.start()

    def stat_go(j, carry):
        to_s, to_h = 2 * lax.div(j, head_n) + h, lax.rem(j, head_n)

        @pl.when((to_s != s) | (to_h != h))
        def _():
            remote(stat_ref, sbuf.at[s], s_send, s_recv, (to_s, to_h)).start()

        return carry

    def stat_wait(sem):
        @pl.when(core == h)
        def _():
            wait_bytes(sbuf.at[pl.ds(0, seq_n - 1)], sem)

        @pl.when(core != h)
        def _():
            wait_bytes(sbuf.at[pl.ds(0, seq_n)], sem)

    lax.fori_loop(0, seq_n, stat_go, 0)

    @pl.when(core == h)
    def _():
        cbuf[0] = ctx_ref[...]
        sbuf[s] = stat_ref[...]

    mod_copy = remote(tmod_ref, mbuf, m_send.at[1], m_recv.at[1], sibling)
    for copy in small[5:]:
        copy.wait()
    mod_copy.start()

    def weight_of(ref, hh):
        return jnp.concatenate(
            [ref[:, pl.ds(pl.multiple_of(i * width + hh * HD, HD), HD)] for i in range(2)], axis=1
        )

    def c_wait(i):
        remote(ctx_ref, cbuf.at[i], c_send.at[0], c_recv.at[i], (there, h)).wait_recv()

    def text_piece(xx, zz):
        hh = 2 * zz + xx
        out = None
        for i, ref in enumerate((wt_ref, wbuf)):
            w = weight_of(ref, hh)
            term = dot_f32(lhs_ref[2 * i], w) + dot_f32(lhs_ref[2 * i + 1], w)
            out = term if out is None else out + term
        return out

    ways = [z_n // 2] + [dz for dz in range(1, z_n) if dz != z_n // 2] + [0]

    def peer_of(i):
        return lax.rem(z + ways[i], z_n)

    def tx_copy(i):
        peer = peer_of(i)
        return remote(tstage.at[peer], txbuf.at[peer], tx_send, tx_recv.at[i], across)

    def text_out(i):
        peer = peer_of(i)
        tstage[peer] = text_piece(1 - x, peer).astype(jnp.bfloat16)
        tx_copy(i).start()

    def text_begin():
        mod_copy.wait_recv()
        w_copy.wait_recv()
        for i, mods in enumerate((tmod_ref, mbuf)):
            tokens_here = jnp.transpose(cbuf[i].astype(jnp.float32))
            tokens_here = tokens_here - jnp.mean(tokens_here, axis=1, keepdims=True)
            high, low = split_high_low(tokens_here * (1.0 + mods[1:2, :]))
            lhs_ref[2 * i] = high
            lhs_ref[2 * i + 1] = low
        for i in range(z_n):
            text_out(i)

    g_arrive()
    sums = group_sum(jnp.sum(gbuf[...], axis=0), per_group) / cell_count
    mean = sums[:lines]
    scale = lax.rsqrt(sums[lines:] - mean * mean + eps_norm)
    mean = jnp.concatenate([mean[j : j + 1] for j in range(lines)], axis=1)
    scale = jnp.concatenate([scale[j : j + 1] for j in range(lines)], axis=1)
    normed = (values - mean) * scale * gain_ref[...] + bias_ref[...]
    active = normed / (1.0 + jnp.exp(-normed))
    frame = lax.rem(lax.broadcasted_iota(jnp.int32, active.shape, 0), frames)
    back_one = jnp.where(frame == 0, active, pltpu.roll(active, 1, 0))
    back_two = jnp.where(frame < 2, jnp.where(frame == 0, active, back_one), pltpu.roll(active, 2, 0))
    taps = convw_ref.shape[0] // 3
    shares = sum(
        dot_minor(part.astype(jnp.bfloat16), convw_ref[a * taps : (a + 1) * taps, :])
        for a, part in enumerate((back_two, back_one, active))
    )
    line = shares.shape[0] // 2
    tap = taps // 3

    def share_of(row, b):
        piece = shares[row * line : (row + 1) * line, b * tap : (b + 1) * tap]
        return jnp.concatenate([piece, jnp.zeros((line, 128 - tap), jnp.float32)], axis=1)

    zown[0] = share_of(0, 2)
    zown[1] = share_of(0, 1) + share_of(1, 2)
    zown[2] = share_of(0, 0) + share_of(1, 1)
    zown[3] = share_of(1, 0)

    def rim(src, dst, i, device):
        return remote(src, dst, h_send.at[i], h_recv.at[i], device)

    up = [rim(zown.at[0], zhigh.at[i], i, (s - 1, (h, 1 - h)[i])) for i in range(2)]
    down = [rim(zown.at[3], zlow.at[i], 2 + i, (s + 1, (h, 1 - h)[i])) for i in range(2)]
    side = rim(zown.at[pl.ds(1, 2)], zside, 4, (s, 1 - h))

    @pl.when(s > 0)
    def _():
        for copy in up:
            copy.start()

    @pl.when(s < seq_n - 1)
    def _():
        for copy in down:
            copy.start()

    side.start()

    @pl.when(s == 0)
    def _():
        zlow[...] = jnp.zeros_like(zlow)

    @pl.when(s == seq_n - 1)
    def _():
        zhigh[...] = jnp.zeros_like(zhigh)

    @pl.when(core == h)
    def _():
        c_wait(1)
        text_begin()

    fx_copy.wait_recv()

    def fold_sum(zz):
        return fold_pair(x, zz) + fxbuf[zz].astype(jnp.float32)

    for dz in range(1, z_n):
        peer = lax.rem(z + dz, z_n)
        fzsend[peer] = fold_sum(peer).astype(fzsend.dtype)
        remote(
            fzsend.at[peer],
            fzbuf.at[dz],
            fz_send,
            fz_recv,
            (peer * NEAR + lax.rem(s, NEAR), h),
        ).start()

    mod_at = lax.broadcasted_iota(jnp.int32, (8, depth), 0)
    coef_lhs = jnp.where(mod_at == 0, 1.0 + tmod_ref[1:2, :], jnp.where(mod_at == 1, tmod_ref[0:1, :], 0.0))
    coef_lhs = jnp.concatenate(split_high_low(coef_lhs), axis=0)

    for hh in range(heads_here):
        product = dot_f32(coef_lhs, weight_of(wt_ref, hh))
        coef[hh] = product[0:2] + product[8:10]
    kbuf[s] = coef[chip]

    def coef_go(j, carry):
        @pl.when(j != s)
        def _():
            remote(coef.at[lax.div(j, 2)], kbuf.at[s], k_send, k_recv, (j, h)).start()

        return carry

    lax.fori_loop(0, seq_n, coef_go, 0)

    @pl.when(core != h)
    def _():
        c_wait(0)
        c_wait(1)
        text_begin()

    @pl.when(s < seq_n - 1)
    def _():
        for copy in up:
            copy.wait_recv()

    @pl.when(s > 0)
    def _():
        for copy in down:
            copy.wait_recv()

    side.wait_recv()
    blocks = []
    lane = lanes_of((8, 128))
    conv_bias = jnp.concatenate([convb_ref[...], jnp.zeros((1, 112), jnp.float32)], axis=1)
    for row in range(2):
        rims = zlow if row == 0 else zhigh
        mine = zown[1 + row] + rims[0]
        other = zside[row] + rims[1]
        cols = [mine[8 * i : 8 * i + 8] for i in range(line // 8)]
        left = jnp.where(h == 1, other[line - 8 : line], 0.0)
        right = jnp.where(h == 0, other[0:8], 0.0)
        cols = [left] + cols + [right]
        for i in range(line // 8):
            got = cols[i] + pltpu.roll(cols[i + 1], 128 - 16, 1) + pltpu.roll(cols[i + 2], 128 - 32, 1)
            got = jnp.where(lane < 16, got + conv_bias, 0.0)
            at = 16 * (2 * row + i % 2)
            blocks.append(got if at == 0 else pltpu.roll(got, at, 1))
    per_row = line // 8
    tokens = [
        blocks[2 * q] + blocks[2 * q + 1] + blocks[per_row + 2 * q] + blocks[per_row + 2 * q + 1]
        for q in range(per_row // 2)
    ]
    patches = jnp.concatenate(tokens, axis=0).astype(jnp.bfloat16)
    hidden = dot_f32(patches[:, : pw_ref.shape[0]], pw_ref[...]) + pb_ref[...]
    center = jnp.mean(hidden, axis=1, keepdims=True)
    offset = hidden - center
    spread_of = jnp.mean(offset * offset, axis=1, keepdims=True)
    rstd = lax.rsqrt(spread_of + eps_norm)
    hidden_ref[...] = hidden
    r_high = rstd.astype(jnp.bfloat16).astype(jnp.float32)
    r_mid = (rstd - r_high).astype(jnp.bfloat16).astype(jnp.float32)
    r_low = rstd - r_high - r_mid
    lane = lanes_of((own_rows, 128))
    block = patches.astype(jnp.float32)
    for at, value in ((64, jnp.ones_like(rstd)), (65, r_high), (66, r_mid), (67, r_low)):
        block = jnp.where(lane == at, value, block)
    psrc[...] = block.astype(jnp.bfloat16)
    pbuf[my_same] = psrc[...]
    p_begin()

    wout_copy.start()

    def tz_copy(dz):
        peer = lax.rem(z + dz, z_n)
        return remote(
            tzsend.at[peer],
            tzbuf.at[dz],
            tz_send,
            tz_recv,
            (peer * NEAR + lax.rem(s, NEAR), h),
        )

    def text_sum(i):
        peer = peer_of(i)
        mine = text_piece(x, peer)
        tx_copy(i).wait_recv()
        return mine + txbuf[peer].astype(jnp.float32)

    def text_on(i):
        tzsend[peer_of(i)] = text_sum(i).astype(jnp.bfloat16)
        tz_copy(ways[i]).start()

    text_on(0)
    text_on(1)

    for i in range(2, z_n - 1):
        text_on(i)

    wait_bytes(fzbuf.at[pl.ds(1, z_n - 1)], fz_recv)
    fold_half = fold_sum(z)
    for dz in range(1, z_n):
        fold_half = fold_half + fzbuf[dz].astype(jnp.float32)
    ffull[half_rows(core), :] = fold_half
    fold_copy = remote(
        ffull.at[half_rows(core), :], ffull.at[half_rows(core), :], m_send.at[4], m_recv.at[4], sibling
    )
    fold_copy.start()
    remote(
        ffull.at[half_rows(core), :], ffull.at[half_rows(1 - core), :], m_send.at[4], m_recv.at[4], sibling
    ).wait_recv()
    fold = ffull[...]
    shift = fold[68:69, :]
    row_at = lax.broadcasted_iota(jnp.int32, fold.shape, 0)
    fold_high, fold_low = split_high_low(jnp.where(row_at < 65, fold, 0.0))
    p_arrive()
    all_tokens = pbuf[...].reshape(same_n * own_rows, 128)
    tail = all_tokens[:, 64:].astype(jnp.float32)
    scale_of = tail[:, 1:2] + tail[:, 2:3] + tail[:, 3:4]
    tokens_in = all_tokens[:, : fold.shape[0]]
    qkv = (dot_f32(tokens_in, fold_high) + dot_f32(tokens_in, fold_low)) * scale_of + shift
    qkv = qkv.astype(jnp.bfloat16)
    query = qkv[:, :HD]
    ikv[core] = qkv[:, HD:]
    image_copy = remote(ikv.at[core], ikv.at[core], m_send.at[6], m_recv.at[6], sibling)
    image_copy.start()
    pair = head_n * own_rows

    text_own = text_sum(z_n - 1)
    stat_wait(s_recv)
    wait_bytes(kbuf.at[pl.ds(0, seq_n - 1)], k_recv)
    text_sums = jnp.sum(sbuf[...], axis=0)
    sum_at = lax.broadcasted_iota(jnp.int32, (8, half), 0)
    text_sums = jnp.where(sum_at == 0, text_sums[0:1], text_sums[1:2])
    text_sums = jnp.transpose(text_sums) / width_full
    text_mean = text_sums[:, 0:1]
    text_scale = lax.rsqrt(text_sums[:, 1:2] - text_mean * text_mean + eps_norm)
    means_apart = sbuf[...][:, 0, :] / depth - jnp.sum(sbuf[...], axis=0)[0:1] / width_full
    coefs = kbuf[...]
    centred_off = jnp.dot(
        jnp.transpose(means_apart),
        coefs[:, 0, :],
        preferred_element_type=jnp.float32,
        precision=lax.Precision.HIGHEST,
    )
    text_shift = jnp.sum(coefs, axis=0)[1:2]

    def attend(scores, values_of):
        top = jnp.max(scores, axis=1, keepdims=True)
        probs = jnp.exp(scores - top)
        return top, jnp.sum(probs, axis=1, keepdims=True), dot_f32(probs.astype(jnp.bfloat16), values_of)

    remote(ikv.at[core], ikv.at[1 - core], m_send.at[6], m_recv.at[6], sibling).wait_recv()
    image_kv = ikv[...].reshape(-1, 2 * HD)
    image_scores = dot_minor(query, image_kv[:, :HD]) / HD
    image_top, image_total, image_part = attend(image_scores, image_kv[:, HD:])

    wait_bytes(tzbuf.at[pl.ds(1, z_n - 1)], tz_recv)
    for dz in range(1, z_n):
        text_own = text_own + tzbuf[dz].astype(jnp.float32)
    text_own = (text_own + centred_off) * text_scale + text_shift
    tkv[core] = text_own.astype(jnp.bfloat16)
    text_copy = remote(tkv.at[core], tkv.at[core], m_send.at[5], m_recv.at[5], sibling)
    text_copy.start()
    remote(tkv.at[core], tkv.at[1 - core], m_send.at[5], m_recv.at[5], sibling).wait_recv()
    text_kv = tkv[...].reshape(-1, 2 * HD)
    text_scores = dot_minor(query, text_kv[:, :HD]) / HD
    text_scores = jnp.where(lanes_of(text_scores.shape) < len_ref[0], text_scores, -1e30)
    text_top, text_total, text_part = attend(text_scores, text_kv[:, HD:])
    top = jnp.maximum(image_top, text_top)
    image_share, text_share = jnp.exp(image_top - top), jnp.exp(text_top - top)
    totals = image_total * image_share + text_total * text_share
    attended = (image_part * image_share + text_part * text_share) / totals
    attended = attended.astype(jnp.bfloat16)
    attsend[...] = attended.reshape(heads_here, pair, HD)

    def a_copy(k, owner):
        return remote(
            attsend.at[k],
            attrecv.at[:, pl.ds(pl.multiple_of(owner * HD, HD), HD)],
            a_send,
            a_recv,
            (2 * k + core, h),
        )

    for off in range(1, heads_here):
        a_copy(lax.rem(chip + off, heads_here), chip).start()
    attrecv[:, pl.ds(pl.multiple_of(chip * HD, HD), HD)] = attsend[chip]
    wout_copy.wait()
    wait_bytes(attsend.at[pl.ds(0, heads_here - 1)], a_recv)

    rows = attrecv[...]
    chunks = y_send.shape[0]
    chunk = width_full // chunks

    def y_copy(j):
        at = pl.ds(j * chunk, chunk)
        return remote(
            ysend.at[:, at], yrecv.at[:, at], y_send.at[j], y_recv.at[j], (s, 1 - h)
        )

    for j in range(chunks):
        part = dot_f32(rows, woutv[:, j * chunk : (j + 1) * chunk])
        first, second = part[:own_rows], part[own_rows:]
        ysend[:, j * chunk : (j + 1) * chunk] = jnp.where(h == 0, second, first).astype(jnp.bfloat16)
        proj[:, j * chunk : (j + 1) * chunk] = jnp.where(h == 0, first, second)
        y_copy(j).start()
    def out_copy(j):
        at = pl.ds(j * chunk, chunk)
        return pltpu.make_async_copy(out_ref.at[:, at], out_hbm.at[:, at], out_sem.at[j])

    g_sent()
    p_sent()

    stat_wait(s_send)
    wait_bytes(kbuf.at[pl.ds(0, seq_n - 1)], k_send)
    far_copy.wait_send()

    @pl.when(core != h)
    def _():
        near_copy.wait_send()

    for copy in (w_copy, mod_copy, pair_copy, fx_copy, fold_copy, image_copy, text_copy, side):
        copy.wait_send()

    @pl.when(s > 0)
    def _():
        for copy in up:
            copy.wait_send()

    @pl.when(s < seq_n - 1)
    def _():
        for copy in down:
            copy.wait_send()

    wait_bytes(fzbuf.at[pl.ds(0, z_n - 1)], fz_send)
    wait_bytes(tzbuf.at[pl.ds(0, z_n - 1)], tz_send)
    wait_bytes(tstage, tx_send)
    wait_bytes(attsend.at[pl.ds(0, heads_here - 1)], a_send)
    for j in range(chunks):
        y_copy(j).wait_recv()
        at = slice(j * chunk, (j + 1) * chunk)
        projected = proj[:, at] + yrecv[:, at].astype(jnp.float32) + ob_ref[:, at]
        out_ref[:, at] = (hidden_ref[:, at] + mod_ref[2:3, at] * projected).astype(jnp.bfloat16)
        out_copy(j).start()
    for j in range(chunks):
        y_copy(j).wait_send()
        out_copy(j).wait()


def fused_body(
    features,
    gn_gain,
    gn_bias,
    conv_weight,
    conv_bias,
    patch_weight,
    patch_bias,
    image_mod,
    w_qkv,
    text_ids,
    text_length,
    text_table,
    text_mod,
    w_text,
    w_out,
    out_bias,
):
    frame_count, row_count, col_count, chan_count = features.shape
    width_full = patch_weight.shape[1]
    seq_n, head_n = lax.axis_size("seq"), lax.axis_size("head")
    depth, _, head_width = w_qkv.shape
    heads_here = head_width // HD
    z_n = seq_n // NEAR
    cells = frame_count * row_count * col_count
    own = cells // 4
    half = text_ids.shape[0] // 2
    count = seq_n * head_n
    f32, bf16 = jnp.float32, jnp.bfloat16

    anywhere = pl.BlockSpec(memory_space=pl.ANY)
    sems = pltpu.SemaphoreType.DMA
    scratch = pltpu.VMEM
    line = cells // 2
    fold_shape = (48, 3 * HD)
    out = pl.pallas_call(
        functools.partial(fused_kernel, seq_n, head_n, cells * (chan_count // GN_GROUPS) * count),
        out_shape=jax.ShapeDtypeStruct((own, width_full), bf16),
        in_specs=[anywhere, pl.BlockSpec(memory_space=pltpu.SMEM)] + [anywhere] * 14,
        out_specs=anywhere,
        scratch_shapes=[
            scratch((depth, 2 * head_width), bf16),
            scratch((own, width_full), bf16),
            scratch(features.shape, bf16),
            scratch(patch_weight.shape, bf16),
            scratch((1, width_full), f32),
            scratch(image_mod.shape, f32),
            scratch((1, text_ids.shape[0]), jnp.int32),
            scratch((1, chan_count), f32),
            scratch((1, chan_count), f32),
            scratch((27 * conv_bias.shape[0], chan_count), bf16),
            scratch((1, conv_bias.shape[0]), f32),
            scratch(text_mod.shape, f32),
            scratch((1, width_full), f32),
            scratch((cells, chan_count), f32),
            scratch((depth, text_table.shape[1]), bf16),
            scratch((3, depth, head_width), bf16),
            scratch((depth, half), bf16),
            scratch((2, half), f32),
            scratch((8, 128), f32),
            scratch((count, 8, 128), f32),
            scratch((4, line, 128), f32),
            scratch((2, line, 128), f32),
            scratch((2, line, 128), f32),
            scratch((2, line, 128), f32),
            scratch((own, 128), bf16),
            scratch((count // 2, own, 128), bf16),
            scratch((seq_n, 2, half), f32),
            scratch((heads_here, 2, 2 * HD), f32),
            scratch((seq_n, 2, 2 * HD), f32),
            scratch((2, depth, half), bf16),
            scratch((depth, 2 * head_width), bf16),
            scratch((2, depth), f32),
            scratch((4, half, depth), bf16),
            scratch((heads_here, 2 * fold_shape[0], 3 * HD), f32),
            scratch((heads_here, *fold_shape), f32),
            scratch((z_n, *fold_shape), bf16),
            scratch((z_n, *fold_shape), bf16),
            scratch((z_n, *fold_shape), bf16),
            scratch((z_n, *fold_shape), bf16),
            scratch((2 * fold_shape[0], 3 * HD), f32),
            scratch((z_n, half, 2 * HD), bf16),
            scratch((z_n, half, 2 * HD), bf16),
            scratch((z_n, half, 2 * HD), bf16),
            scratch((z_n, half, 2 * HD), bf16),
            scratch((2, half, 2 * HD), bf16),
            scratch((2, count * own // 2, 2 * HD), bf16),
            scratch((heads_here, head_n * own, HD), bf16),
            scratch((head_n * own, head_width), bf16),
            scratch((own, width_full), f32),
            scratch((own, width_full), bf16),
            scratch((own, width_full), bf16),
            scratch((own, width_full), f32),
            scratch((head_width, width_full), bf16),
            sems((12,)),
            sems((4,)),
            sems((8,)),
            sems,
            sems,
            sems,
            sems,
            sems,
            sems,
            sems,
            sems,
            sems,
            sems,
            sems((2,)),
            sems((2,)),
            sems((7,)),
            sems((7,)),
            sems((5,)),
            sems((5,)),
            sems,
            sems,
            sems,
            sems((z_n,)),
            sems,
            sems,
            sems,
            sems,
            sems((4,)),
            sems((4,)),
        ],
        compiler_params=pltpu.CompilerParams(
            collective_id=3, has_side_effects=True, vmem_limit_bytes=60 * 1024 * 1024
        ),
    )(
        w_text.reshape(depth, 2 * head_width),
        text_length,
        features,
        patch_weight,
        patch_bias[None],
        image_mod,
        text_ids[None],
        gn_gain[None],
        gn_bias[None],
        conv_weight.reshape(-1, chan_count),
        conv_bias[None],
        text_mod,
        out_bias[None],
        text_table,
        w_qkv.transpose(1, 0, 2),
        w_out,
    )
    out = out.reshape(col_count // 2, frame_count, width_full).transpose(1, 0, 2)
    return out.reshape(frame_count, row_count // 2, col_count // 2, width_full)


def choose_body(*operands):
    features, w_qkv = operands[0], operands[8]
    seq_n, head_n = lax.axis_size("seq"), lax.axis_size("head")
    pair = seq_n == 2 * (w_qkv.shape[2] // HD) and head_n == 2 and seq_n % NEAR == 0
    small = features.shape[:3] == (8, 2, 4) and features.shape[3] == 512
    return fused_body(*operands) if pair and small else body(*operands)


def solution(mesh):
    return jax.shard_map(
        choose_body,
        mesh=mesh,
        in_specs=(
            P(None, "seq", "head", None),
            P(),
            P(),
            P(),
            P(),
            P(),
            P(),
            P(),
            P("seq", None, "head"),
            P(),
            P(),
            P("seq", None),
            P(None, "seq"),
            P("seq", None, "head"),
            P("head", None),
            P(),
        ),
        out_specs=P(None, "seq", "head", None),
        check_vma=False,
    )
```
